32 devices in a mesh: slab: 8 (over y, x, core), grp: 4 (over z).
Axes of the slice: x: 2, y: 2, z: 4, core: 2. Of those that a mesh axis runs over, the one named last changes fastest.
Arguments:
- volume: float32 [64, 32, 16, 128], P(None, 'slab', 'grp'), may hold values from -6 to 6
- conv_fine: float32 [3, 3, 3, 64, 64], replicated, may hold values from -0.15625 to 0.15625
- down_first: float32 [2, 2, 2, 64, 128], replicated, may hold values from -0.25 to 0.25
- conv_middle: float32 [3, 3, 3, 128, 128], replicated, may hold values from -0.109375 to 0.109375
- down_second: float32 [2, 2, 2, 128, 256], P(None, None, None, None, 'grp'), may hold values from -0.1875 to 0.1875
- conv_coarse: float32 [3, 3, 3, 256, 512], P(None, None, None, None, 'grp'), may hold values from -0.078125 to 0.078125
Outputs:
- features: float32 [512, 8, 128], P('grp', 'slab')
The draws below stay inside these ranges and needn't reach their ends.
All inputs are finite; a program needn't handle non-finite values.
Results may differ from the reference program's by a relative error of at most 0.000082.
Values sent between devices are 32-bit elements; how exact they have to be, the bound alone decides.
A program may use at most 64 MiB of HBM per device.

```python
import jax
import jax.numpy as jnp
from jax import lax

C1 = 64
C2 = 128
C3 = 256
C4 = 512
WIDTH = 128
DEPTH = 32
HEIGHT = 16


def shard_levels(key, dims, pieces, low, largest):
    factor_of = 1.0
    for dim, parts in pieces:
        steps = jax.random.uniform(jax.random.fold_in(jax.random.fold_in(key, 6), dim), (parts,), jnp.float32, low / len(pieces), largest / len(pieces))
        factor_of = factor_of * jnp.repeat(jnp.exp(steps), dims[dim] // parts).reshape((-1,) + (1,) * (len(dims) - 1 - dim))
    return factor_of


def scatter_about(own_key, extent, deviation, reach, pieces=(), dtype=jnp.bfloat16):
    values = deviation * jax.random.normal(own_key, extent, jnp.float32)
    if pieces:
        values = values * shard_levels(own_key, extent, pieces, -0.22, 0.18)
    return jnp.clip(values, -reach, reach).astype(dtype)


def setup_inputs(seed: int = 0) -> dict:
    keys = jax.random.split(jax.random.key(seed), 7)
    volume = scatter_about(keys[0], (C1, DEPTH, HEIGHT, WIDTH), 1.0, 6.0, ((1, 8), (2, 4)), jnp.float32)
    conv_fine = scatter_about(keys[1], (3, 3, 3, C1, C1), (27 * C1) ** -0.5, 0.15625, (), jnp.float32)
    down_first = scatter_about(keys[2], (2, 2, 2, C1, C2), (8 * C1) ** -0.5, 0.25, (), jnp.float32)
    conv_middle = scatter_about(keys[3], (3, 3, 3, C2, C2), (27 * C2) ** -0.5, 0.109375, (), jnp.float32)
    down_second = scatter_about(keys[4], (2, 2, 2, C2, C3), (8 * C2) ** -0.5, 0.1875, ((4, 4),), jnp.float32)
    conv_coarse = scatter_about(keys[5], (3, 3, 3, C3, C4), (27 * C3) ** -0.5, 0.078125, ((4, 4),), jnp.float32)
    return {"volume": volume, "conv_fine": conv_fine, "down_first": down_first, "conv_middle": conv_middle, "down_second": down_second, "conv_coarse": conv_coarse}


def convolve(field, kernel, stride, padding):
    return lax.conv_general_dilated(field[None], kernel, (stride, stride, stride), padding, dimension_numbers=("NCDHW", "DHWIO", "NCDHW"), precision=lax.Precision.HIGHEST)[0]


def reference(volume, conv_fine, down_first, conv_middle, down_second, conv_coarse):
    same = ((1, 1), (1, 1), (1, 1))
    valid = ((0, 0), (0, 0), (0, 0))
    level_one = jax.nn.gelu(convolve(volume, conv_fine, 1, same), approximate=False)
    level_two = convolve(level_one, down_first, 2, valid)
    level_two = jax.nn.gelu(convolve(level_two, conv_middle, 1, same), approximate=False)
    coarse = convolve(level_two, down_second, 2, valid)
    result = jax.nn.gelu(convolve(coarse, conv_coarse, 1, same), approximate=False)
    return result.reshape(C4, DEPTH // 4, (HEIGHT // 4) * (WIDTH // 4))
```

```python
import functools

import jax
import jax.numpy as jnp
from jax import lax
from jax.experimental import pallas as pl
from jax.experimental.pallas import tpu as pltpu
from jax.sharding import PartitionSpec as P

MESH = pl.DeviceIdType.MESH
F32, BF16 = jnp.float32, jnp.bfloat16
WAYS = ((1, 0), (-1, 0), (0, 1), (0, -1), (1, 1), (1, -1), (-1, 1), (-1, -1))


def split(x):
    high = x.astype(BF16)
    return high, (x - high.astype(F32)).astype(BF16)


def stacked(x):
    return jnp.concatenate(split(x), axis=0)


def product(both, weights, dims=(((1,), (0,)), ((), ()))):
    dot = functools.partial(lax.dot_general, dimension_numbers=dims, preferred_element_type=F32)
    rows = both.shape[0] // 2
    wide = dot(both, weights[0])
    return wide[:rows] + wide[rows:] + dot(both[:rows], weights[1])


def plus(total, term):
    return term if total is None else total + term


def gelu(x):
    return 0.5 * x * (1.0 + lax.erf(x * (0.5**0.5)))


def beside(x, span):
    at = lax.rem(lax.broadcasted_iota(jnp.int32, x.shape, 0), span)
    before = jnp.where(at == 0, 0.0, pltpu.roll(x, 1, 0))
    after = jnp.where(at == span - 1, 0.0, pltpu.roll(x, x.shape[0] - 1, 0))
    return before, after


def kernel(
    slabs, groups,
    vol_hbm, fine_hbm, down1_hbm, middle_hbm, shard, coarse_hbm,
    out,
    vol, fine, field, pair, rows, fine_h, fine_l, down1, down1_h, down1_l, middle, middle_h, middle_l,
    second, rows2, level2, gathered, coarse_w, edges_h, edges_l, centre_h, centre_l,
    coarse, taps, upward, downward, from_lower, from_upper,
    load_sem, send1, recv1, send2, recv2, wsend, wrecv, xsend, xrecv, fsend, frecv, csend, crecv, psend, precv,
):
    s, g = lax.axis_index("slab"), lax.axis_index("grp")
    depth, height, chans, width = (field.shape[0] - 2, field.shape[1] - 2) + field.shape[2:]
    half = width // 2

    loads = [
        pltpu.make_async_copy(vol_hbm, vol, load_sem.at[3]),
        pltpu.make_async_copy(fine_hbm, fine, load_sem.at[4]),
        pltpu.make_async_copy(shard, gathered.at[g], load_sem.at[5]),
        pltpu.make_async_copy(down1_hbm, down1, load_sem.at[0]),
        pltpu.make_async_copy(middle_hbm, middle, load_sem.at[1]),
        pltpu.make_async_copy(coarse_hbm, coarse_w, load_sem.at[2]),
    ]
    for load in loads:
        load.start()

    def exists(ds, dg):
        return (s + ds >= 0) & (s + ds < slabs) & (g + dg >= 0) & (g + dg < groups)

    barrier = pltpu.get_barrier_semaphore()
    heard = jnp.int32(0)
    for ds, dg in WAYS:
        there = exists(ds, dg)
        heard = heard + there.astype(jnp.int32)

        @pl.when(there)
        def _():
            pl.semaphore_signal(barrier, inc=1, device_id=(s + ds, g + dg), device_id_type=MESH)

    for dg in range(2, groups):
        for sign in (1, -1):
            there = exists(0, sign * dg)
            heard = heard + there.astype(jnp.int32)

            @pl.when(there)
            def _():
                pl.semaphore_signal(barrier, inc=1, device_id=(s, g + sign * dg), device_id_type=MESH)

    sibling = s + 1 - 2 * lax.rem(s, 2)
    place = lax.rem(s // 2, 2)
    crossings = [s + 2 - 4 * place]
    for peer in crossings:
        pl.semaphore_signal(barrier, inc=1, device_id=(peer, g), device_id_type=MESH)
    loads[0].wait()
    lines = depth * height
    for r in range(lines):
        field[1 + r // height, 1 + r % height] = vol[pl.ds(r, chans, stride=lines), :]
    pl.semaphore_wait(barrier, heard + len(crossings))

    def part(way, size, offset):
        if way == 0:
            return pl.ds(offset, size)
        return pl.ds(offset + (size - 1 if way > 0 else 0), 1)

    def landing(way, size):
        if way == 0:
            return pl.ds(1, size)
        return pl.ds(0 if way > 0 else size + 1, 1)

    def halo(src, offset, buf, sends, recvs):
        nd, nh = buf.shape[0] - 2, buf.shape[1] - 2
        copies = []
        for k, (ds, dg) in enumerate(WAYS):
            copies.append(
                pltpu.make_async_remote_copy(
                    src_ref=src.at[part(ds, nd, offset), part(dg, nh, offset)],
                    dst_ref=buf.at[landing(ds, nd), landing(dg, nh)],
                    send_sem=sends.at[k],
                    recv_sem=recvs.at[k],
                    device_id=(s + ds, g + dg),
                    device_id_type=MESH,
                )
            )

            @pl.when(exists(ds, dg))
            def _():
                copies[k].start()

            @pl.when(jnp.logical_not(exists(-ds, -dg)))
            def _():
                piece = (landing(ds, nd), landing(dg, nh))
                shape = (piece[0].size, piece[1].size) + buf.shape[2:]
                buf[piece[0], piece[1]] = jnp.zeros(shape, F32)

        return copies

    def arrive(copies, received, ways=range(len(WAYS))):
        for k in ways:
            ds, dg = WAYS[k]
            if received:
                @pl.when(exists(-ds, -dg))
                def _():
                    copies[k].wait_recv()
            else:
                @pl.when(exists(ds, dg))
                def _():
                    copies[k].wait_send()

    first = halo(field, 1, field, send1, recv1)

    taps_of = shard.shape[0]
    parity = lax.rem(s, 2)
    fourth = pl.ds((parity * 2 + place) * (taps_of // 4), taps_of // 4)
    half_taps = pl.ds(parity * (taps_of // 2), taps_of // 2)
    spread, crossed, forward = [], [], []
    for j in range(1, groups):
        copy = pltpu.make_async_remote_copy(
            src_ref=shard.at[fourth],
            dst_ref=gathered.at[g, fourth],
            send_sem=wsend.at[j],
            recv_sem=wrecv.at[j],
            device_id=(s, lax.rem(g + j, groups)),
            device_id_type=MESH,
        )
        copy.start()
        spread.append(copy)

    def hand_on(arrived, out_copies, piece, sends, recvs, peers):
        for j in range(1, groups):
            for copy in arrived[j - 1]:
                copy.wait_recv()
            source = lax.rem(g + groups - j, groups)
            made = []
            for k, peer in enumerate(peers):
                copy = pltpu.make_async_remote_copy(
                    src_ref=gathered.at[source, piece],
                    dst_ref=gathered.at[source, piece],
                    send_sem=sends.at[j, k],
                    recv_sem=recvs.at[j, k],
                    device_id=(peer, g),
                    device_id_type=MESH,
                )
                copy.start()
                made.append(copy)
            out_copies.append(made)

    loads[1].wait()
    blank = jnp.zeros((chans, 2 * chans), BF16)
    nothing = jnp.zeros((chans, chans), F32)
    for a in range(3):
        for b in range(3):
            for pos in range(4):
                left = fine[(a * 3 + b) * 3 + pos] if pos < 3 else nothing
                right = fine[(a * 3 + b) * 3 + pos - 1] if pos > 0 else nothing
                high, low = split(jnp.concatenate([left, right], axis=1))
                for hb in range(2):
                    p, sub = divmod(b + hb, 2)
                    spot = pl.ds((pos * 2 + sub) * chans, chans)
                    fine_h[a, p, spot, hb * 2 * chans : (hb + 1) * 2 * chans] = high
                    fine_l[a, p, spot, hb * 2 * chans : (hb + 1) * 2 * chans] = low
        for pos in range(4):
            for p, sub, hb in ((0, 0, 1), (1, 1, 0)):
                spot = pl.ds((pos * 2 + sub) * chans, chans)
                fine_h[a, p, spot, hb * 2 * chans : (hb + 1) * 2 * chans] = blank
                fine_l[a, p, spot, hb * 2 * chans : (hb + 1) * 2 * chans] = blank

    pairs = height // 2 + 1
    blocks = height // 2
    d2, h2, c2 = depth // 2, blocks, down1.shape[2]
    for load in loads[2:]:
        load.wait()
    for a in range(2):
        down1_h[a], down1_l[a] = split(down1[a])

    @pl.loop(0, 3)
    def _(a):
        for b in range(3):
            high, low = split(middle[a * 3 + b])
            for hb in range(2):
                spot = pl.ds((b + hb) * 3 * c2, 3 * c2)
                middle_h[a, spot, hb * c2 : (hb + 1) * c2] = high
                middle_l[a, spot, hb * c2 : (hb + 1) * c2] = low

    outs = coarse_w.shape[2]

    @pl.loop(0, 3)
    def _(b):
        for a, k in ((0, 0), (2, 1)):
            high, low = split(coarse_w[a * 3 + b])
            edges_h[b, :, k * outs : (k + 1) * outs] = high
            edges_l[b, :, k * outs : (k + 1) * outs] = low
        centre_h[b], centre_l[b] = split(coarse_w[3 + b])

    def build(p):
        @pl.loop(0, depth + 2)
        def _(d):
            pair[p] = field[d, 2 * p : 2 * p + 2].reshape(2 * chans, width).T
            even = pair[p, pl.ds(0, half, stride=2), :]
            odd = pair[p, pl.ds(1, half, stride=2), :]
            before, _ = beside(odd, half)
            _, after = beside(even, half)
            rows[0, d, p], rows[1, d, p] = split(jnp.concatenate([before, even, odd, after], axis=1))

    totals = [None] * blocks

    def convolve(p):
        for a in range(3):
            lhs = rows[:, a : a + depth, p].reshape(2 * depth * half, 8 * chans)
            for block in range(blocks):
                if 0 <= p - block <= 1:
                    w = (fine_h[a, p - block], fine_l[a, p - block])
                    totals[block] = plus(totals[block], product(lhs, w))

    arrive(first, True, range(0, 2))
    for p in range(1, blocks):
        build(p)
        convolve(p)
    arrive(first, True, range(2, len(WAYS)))
    for p in (0, blocks):
        build(p)
        convolve(p)
    ones = [gelu(t).reshape(d2, 2, half, 4 * chans) for t in totals]
    total = None
    for a in range(2):
        lhs = jnp.concatenate([o[:, a].reshape(d2 * half, 4 * chans) for o in ones], axis=0)
        total = plus(total, product(stacked(lhs), (down1_h[a], down1_l[a])))
    total = total.reshape(h2, d2, half, c2)
    for h in range(h2):
        second[1 : d2 + 1, 1 + h] = total[h]
    again = halo(second, 1, second, send2, recv2)
    hand_on([[c] for c in spread], crossed, fourth, xsend, xrecv, crossings)

    def widen(h):
        @pl.loop(0, d2 + 2)
        def _(d):
            x = second[d, h]
            before, after = beside(x, half)
            spot = slice(h * 3 * c2, (h + 1) * 3 * c2)
            rows2[0, d, :, spot], rows2[1, d, :, spot] = split(jnp.concatenate([before, x, after], axis=1))

    def middle_term(a, low, high, left, right):
        lhs = rows2[:, a : a + d2, :, low:high].reshape(2 * d2 * half, high - low)
        return product(lhs, (middle_h[a, low:high, left:right], middle_l[a, low:high, left:right]))

    k3 = 3 * c2
    arrive(again, True, range(0, 2))
    for h in range(1, h2 + 1):
        widen(h)
    total, sides = None, [None, None]
    for a in range(3):
        total = plus(total, middle_term(a, k3, 3 * k3, 0, 2 * c2))
    arrive(again, True, range(2, len(WAYS)))
    for h in (0, h2 + 1):
        widen(h)
    for a in range(3):
        sides[0] = plus(sides[0], middle_term(a, 0, k3, 0, c2))
        sides[1] = plus(sides[1], middle_term(a, 3 * k3, 4 * k3, c2, 2 * c2))
    hand_on(crossed, forward, half_taps, fsend, frecv, [sibling])
    for h in range(h2):
        level2[h] = gelu(total[:, h * c2 : (h + 1) * c2] + sides[h])
    quarter = half // 2
    lhs = jnp.concatenate(
        [
            level2[h, pl.ds(d * half + c, quarter, stride=2), :]
            for d in range(d2) for h in range(h2) for c in range(2)
        ],
        axis=1,
    )
    lhs = stacked(lhs)
    for made in forward:
        made[0].wait_recv()
    weights = jnp.concatenate(
        [gathered[:, t].reshape(groups * shard.shape[1], c2) for t in range(taps_of)], axis=1
    )
    share = product(lhs, split(weights), (((1,), (1,)), ((), ())))
    coarse[pl.ds(g, 1)] = share[None]
    sent = []
    for j in range(1, groups):
        copy = pltpu.make_async_remote_copy(
            src_ref=coarse.at[g],
            dst_ref=coarse.at[g],
            send_sem=csend.at[j],
            recv_sem=crecv.at[j],
            device_id=(s, lax.rem(g + j, groups)),
            device_id_type=MESH,
        )
        copy.start()
        sent.append(copy)
    cells = groups * quarter
    edge = jnp.zeros((2, quarter, taps.shape[2]), BF16)
    taps[:, 0:quarter] = edge
    taps[:, quarter + cells : 2 * quarter + cells] = edge
    for copy in sent:
        copy.wait_recv()
    x = coarse[...].reshape(cells, coarse.shape[2])
    before, after = beside(x, quarter)
    taps[0, quarter : quarter + cells], taps[1, quarter : quarter + cells] = split(
        jnp.concatenate([before, x, after], axis=1)
    )

    def plane(high, low):
        total = None
        for b in range(3):
            lhs = taps[:, b * quarter : b * quarter + cells].reshape(2 * cells, taps.shape[2])
            total = plus(total, product(lhs, (high[b], low[b])))
        return total

    both = plane(edges_h, edges_l)
    upward[...] = both[:, :outs]
    downward[...] = both[:, outs:]
    up = pltpu.make_async_remote_copy(
        src_ref=upward, dst_ref=from_lower, send_sem=psend.at[0], recv_sem=precv.at[0],
        device_id=(s + 1, g), device_id_type=MESH,
    )
    down = pltpu.make_async_remote_copy(
        src_ref=downward, dst_ref=from_upper, send_sem=psend.at[1], recv_sem=precv.at[1],
        device_id=(s - 1, g), device_id_type=MESH,
    )

    @pl.when(exists(1, 0))
    def _():
        up.start()

    @pl.when(jnp.logical_not(exists(-1, 0)))
    def _():
        from_lower[...] = jnp.zeros(from_lower.shape, F32)

    @pl.when(exists(-1, 0))
    def _():
        down.start()

    @pl.when(jnp.logical_not(exists(1, 0)))
    def _():
        from_upper[...] = jnp.zeros(from_upper.shape, F32)

    centre = plane(centre_h, centre_l)

    @pl.when(exists(-1, 0))
    def _():
        up.wait_recv()

    @pl.when(exists(1, 0))
    def _():
        down.wait_recv()

    out[...] = gelu(centre + from_lower[...] + from_upper[...]).T

    arrive(first, False)
    arrive(again, False)
    for copy in spread + sum(crossed + forward, []) + sent:
        copy.wait_send()

    @pl.when(exists(1, 0))
    def _():
        up.wait_send()

    @pl.when(exists(-1, 0))
    def _():
        down.wait_send()


def per_device(slabs, groups, volume, conv_fine, down_first, conv_middle, down_second, conv_coarse):
    c1, depth, height, width = volume.shape
    c2, c3, c4 = down_first.shape[4], conv_coarse.shape[3], conv_coarse.shape[4]
    half, quarter = width // 2, width // 4
    d2, h2 = depth // 2, height // 2
    part = down_second.shape[4]
    cells = groups * quarter
    vol = volume.reshape(c1 * depth * height, width)
    fine = conv_fine.reshape(27, c1, c1)
    down1 = down_first.reshape(2, 4 * c1, c2)
    middle = conv_middle.reshape(9, 3 * c2, c2)
    shard = jnp.swapaxes(down_second, 3, 4).reshape(8, part, c2)
    pairs = h2 + 1
    coarse_w = conv_coarse.reshape(9, 3 * c3, c4)
    V = pltpu.VMEM
    vmem, away = pl.BlockSpec(memory_space=pltpu.VMEM), pl.BlockSpec(memory_space=pl.ANY)
    dma = pltpu.SemaphoreType.DMA
    result = pl.pallas_call(
        functools.partial(kernel, slabs, groups),
        out_shape=pltpu.VMEM((c4, cells), F32),
        in_specs=[away] * 6,
        out_specs=vmem,
        scratch_shapes=[
            V(vol.shape, F32),
            V(fine.shape, F32),
            V((depth + 2, height + 2, c1, width), F32),
            V((pairs, width, 2 * c1), F32),
            V((2, depth + 2, pairs, half, 8 * c1), BF16),
            V((3, 2, 8 * c1, 4 * c1), BF16),
            V((3, 2, 8 * c1, 4 * c1), BF16),
            V(down1.shape, F32),
            V(down1.shape, BF16),
            V(down1.shape, BF16),
            V(middle.shape, F32),
            V((3, 12 * c2, 2 * c2), BF16),
            V((3, 12 * c2, 2 * c2), BF16),
            V((d2 + 2, h2 + 2, half, c2), F32),
            V((2, d2 + 2, half, 12 * c2), BF16),
            V((h2, d2 * half, c2), F32),
            V((groups,) + shard.shape, F32),
            V(coarse_w.shape, F32),
            V((3, 3 * c3, 2 * c4), BF16),
            V((3, 3 * c3, 2 * c4), BF16),
            V((3, 3 * c3, c4), BF16),
            V((3, 3 * c3, c4), BF16),
            V((groups, quarter, c3), F32),
            V((2, cells + 2 * quarter, 3 * c3), BF16),
            V((cells, c4), F32),
            V((cells, c4), F32),
            V((cells, c4), F32),
            V((cells, c4), F32),
            dma((6,)),
            dma((8,)), dma((8,)), dma((8,)), dma((8,)),
            dma((groups,)), dma((groups,)), dma((groups, 3)), dma((groups, 3)), dma((groups, 1)), dma((groups, 1)), dma((groups,)), dma((groups,)),
            dma((2,)), dma((2,)),
        ],
        compiler_params=pltpu.CompilerParams(
            collective_id=0, has_side_effects=True, vmem_limit_bytes=60 * 1024 * 1024
        ),
    )(vol, fine, down1, middle, shard, coarse_w)
    return result.reshape(c4, 1, cells)


def solution(mesh):
    placed = (
        P(None, "slab", "grp", None),
        P(),
        P(),
        P(),
        P(None, None, None, None, "grp"),
        P(None, None, None, None, "grp"),
    )
    body = functools.partial(per_device, mesh.shape["slab"], mesh.shape["grp"])
    return jax.shard_map(
        body, mesh=mesh, in_specs=placed, out_specs=P("grp", "slab", None), check_vma=False
    )
```

```python
import functools

import jax
import jax.numpy as jnp
from jax import lax
from jax.experimental import pallas as pl
from jax.experimental.pallas import tpu as pltpu
from jax.sharding import PartitionSpec as P

MESH = pl.DeviceIdType.MESH
F32, BF16 = jnp.float32, jnp.bfloat16
WAYS = ((1, 0), (-1, 0), (0, 1), (0, -1), (1, 1), (1, -1), (-1, 1), (-1, -1))


def split(x):
    high = x.astype(BF16)
    return high, (x - high.astype(F32)).astype(BF16)


def stacked(x):
    return jnp.concatenate(split(x), axis=0)


def product(both, weights, dims=(((1,), (0,)), ((), ()))):
    dot = functools.partial(lax.dot_general, dimension_numbers=dims, preferred_element_type=F32)
    rows = both.shape[0] // 2
    wide = dot(both, weights[0])
    return wide[:rows] + wide[rows:] + dot(both[:rows], weights[1])


def plus(total, term):
    return term if total is None else total + term


def gelu(x):
    return 0.5 * x * (1.0 + lax.erf(x * (0.5**0.5)))


def apart(x, width, chans):
    lane = lax.broadcasted_iota(jnp.int32, (chans, width), 1)
    before = jnp.where(lane == 0, 0.0, pltpu.roll(x[:chans], 1, 1))
    after = jnp.where(lane == width - 1, 0.0, pltpu.roll(x[2 * chans :], width - 1, 1))
    return before + x[chans : 2 * chans] + after


def beside(x, span):
    at = lax.rem(lax.broadcasted_iota(jnp.int32, x.shape, 0), span)
    before = jnp.where(at == 0, 0.0, pltpu.roll(x, 1, 0))
    after = jnp.where(at == span - 1, 0.0, pltpu.roll(x, x.shape[0] - 1, 0))
    return before, after


def kernel(
    slabs, groups,
    vol_hbm, fine_hbm, down1_hbm, middle_hbm, shard, coarse_hbm,
    out,
    vol, fine, field, field_h, field_l, inner, outer, partial, turned, down1, down1_w, middle, middle_h, middle_l,
    second, rows2, level2, gathered, coarse_w, edges_h, edges_l, centre_h, centre_l,
    coarse, taps, upward, downward, from_lower, from_upper,
    load_sem, send1, recv1, send2, recv2, wsend, wrecv, xsend, xrecv, fsend, frecv, csend, crecv, psend, precv,
):
    s, g = lax.axis_index("slab"), lax.axis_index("grp")
    depth, height, chans, width = (field.shape[0] - 2, field.shape[1] - 2) + field.shape[2:]
    half = width // 2

    loads = [
        pltpu.make_async_copy(vol_hbm, vol, load_sem.at[3]),
        pltpu.make_async_copy(fine_hbm, fine, load_sem.at[4]),
        pltpu.make_async_copy(shard, gathered.at[g], load_sem.at[5]),
        pltpu.make_async_copy(down1_hbm, down1, load_sem.at[0]),
        pltpu.make_async_copy(middle_hbm, middle, load_sem.at[1]),
        pltpu.make_async_copy(coarse_hbm, coarse_w, load_sem.at[2]),
    ]
    for load in loads:
        load.start()

    def exists(ds, dg):
        return (s + ds >= 0) & (s + ds < slabs) & (g + dg >= 0) & (g + dg < groups)

    barrier = pltpu.get_barrier_semaphore()
    heard = jnp.int32(0)
    for ds, dg in WAYS:
        there = exists(ds, dg)
        heard = heard + there.astype(jnp.int32)

        @pl.when(there)
        def _():
            pl.semaphore_signal(barrier, inc=1, device_id=(s + ds, g + dg), device_id_type=MESH)

    for dg in range(2, groups):
        for sign in (1, -1):
            there = exists(0, sign * dg)
            heard = heard + there.astype(jnp.int32)

            @pl.when(there)
            def _():
                pl.semaphore_signal(barrier, inc=1, device_id=(s, g + sign * dg), device_id_type=MESH)

    sibling = s + 1 - 2 * lax.rem(s, 2)
    place = lax.rem(s // 4, 2)
    crossings = [s + 4 - 8 * place]
    for peer in crossings:
        pl.semaphore_signal(barrier, inc=1, device_id=(peer, g), device_id_type=MESH)
    loads[0].wait()
    lines = depth * height
    for r in range(lines):
        field[1 + r // height, 1 + r % height] = vol[pl.ds(r, chans, stride=lines), :]
    pl.semaphore_wait(barrier, heard + len(crossings))

    def part(way, size, offset):
        if way == 0:
            return pl.ds(offset, size)
        return pl.ds(offset + (size - 1 if way > 0 else 0), 1)

    def landing(way, size):
        if way == 0:
            return pl.ds(1, size)
        return pl.ds(0 if way > 0 else size + 1, 1)

    def halo(src, offset, buf, sends, recvs):
        nd, nh = buf.shape[0] - 2, buf.shape[1] - 2
        copies = []
        for k, (ds, dg) in enumerate(WAYS):
            copies.append(
                pltpu.make_async_remote_copy(
                    src_ref=src.at[part(ds, nd, offset), part(dg, nh, offset)],
                    dst_ref=buf.at[landing(ds, nd), landing(dg, nh)],
                    send_sem=sends.at[k],
                    recv_sem=recvs.at[k],
                    device_id=(s + ds, g + dg),
                    device_id_type=MESH,
                )
            )

            @pl.when(exists(ds, dg))
            def _():
                copies[k].start()

            @pl.when(jnp.logical_not(exists(-ds, -dg)))
            def _():
                piece = (landing(ds, nd), landing(dg, nh))
                shape = (piece[0].size, piece[1].size) + buf.shape[2:]
                buf[piece[0], piece[1]] = jnp.zeros(shape, F32)

        return copies

    def arrive(copies, received, ways=range(len(WAYS))):
        for k in ways:
            ds, dg = WAYS[k]
            if received:
                @pl.when(exists(-ds, -dg))
                def _():
                    copies[k].wait_recv()
            else:
                @pl.when(exists(ds, dg))
                def _():
                    copies[k].wait_send()

    first = halo(field, 1, field, send1, recv1)

    taps_of = shard.shape[0]
    parity = lax.rem(s, 2)
    fourth = pl.ds((parity * 2 + place) * (taps_of // 4), taps_of // 4)
    half_taps = pl.ds(parity * (taps_of // 2), taps_of // 2)
    spread, crossed, forward = [], [], []
    for j in range(1, groups):
        copy = pltpu.make_async_remote_copy(
            src_ref=shard.at[fourth],
            dst_ref=gathered.at[g, fourth],
            send_sem=wsend.at[j],
            recv_sem=wrecv.at[j],
            device_id=(s, lax.rem(g + j, groups)),
            device_id_type=MESH,
        )
        copy.start()
        spread.append(copy)

    def hand_on(arrived, out_copies, piece, sends, recvs, peers):
        for j in range(1, groups):
            for copy in arrived[j - 1]:
                copy.wait_recv()
            source = lax.rem(g + groups - j, groups)
            made = []
            for k, peer in enumerate(peers):
                copy = pltpu.make_async_remote_copy(
                    src_ref=gathered.at[source, piece],
                    dst_ref=gathered.at[source, piece],
                    send_sem=sends.at[j, k],
                    recv_sem=recvs.at[j, k],
                    device_id=(peer, g),
                    device_id_type=MESH,
                )
                copy.start()
                made.append(copy)
            out_copies.append(made)

    loads[1].wait()
    blocks = height // 2
    blank = jnp.zeros((3 * chans, chans), BF16)
    wide = jnp.concatenate(
        [
            jnp.concatenate([fine[ab * 3 + c] for c in range(3)], axis=1)
            for ab in range(9)
        ],
        axis=0,
    )
    both = split(wide.T)

    def taps_at(x, b):
        return [x[:, (a * 3 + b) * chans : (a * 3 + b + 1) * chans] for a in range(3)] if 0 <= b < 3 else [blank] * 3

    within = [[n for n in range(4) if 1 <= 2 * block + n <= height] for block in range(blocks)]
    beyond = [(0, 0, 0), (3, 1, 2)]
    for block in range(blocks):
        for hb in range(2):
            parts = []
            for x in both:
                by_line = [taps_at(x, n - hb) for n in within[block]]
                parts.append(jnp.concatenate([line[a] for a in range(3) for line in by_line], axis=1))
            inner[block, hb * 3 * chans : (hb + 1) * 3 * chans] = jnp.concatenate([parts[0], parts[1], parts[0]], axis=1)
    for k, (_, _, b) in enumerate(beyond):
        parts = [jnp.concatenate(taps_at(x, b), axis=1) for x in both]
        outer[k] = jnp.concatenate([parts[0], parts[1], parts[0]], axis=1)
    d2, h2, c2 = depth // 2, blocks, down1.shape[2]
    for load in loads[2:]:
        load.wait()
    for a in range(2):
        for b in range(2):
            for c in range(2):
                spot = pl.ds(((a * 2 + c) * 2 + b) * chans, chans)
                down1_w[spot, 0:c2], down1_w[spot, c2 : 2 * c2] = split(down1[a, (b * 2 + c) * chans : (b * 2 + c + 1) * chans])
    @pl.loop(0, 3)
    def _(a):
        for b in range(3):
            high, low = split(middle[a * 3 + b])
            for hb in range(2):
                spot = pl.ds((b + hb) * 3 * c2, 3 * c2)
                middle_h[a, spot, hb * c2 : (hb + 1) * c2] = high
                middle_l[a, spot, hb * c2 : (hb + 1) * c2] = low

    outs = coarse_w.shape[2]

    @pl.loop(0, 3)
    def _(b):
        for a, k in ((0, 0), (2, 1)):
            high, low = split(coarse_w[a * 3 + b])
            edges_h[b, :, k * outs : (k + 1) * outs] = high
            edges_l[b, :, k * outs : (k + 1) * outs] = low
        centre_h[b], centre_l[b] = split(coarse_w[3 + b])

    def narrow(ds, hs):
        field_h[ds, hs], field_l[ds, hs] = split(field[ds, hs])

    def across(first, count, d):
        columns = []
        for e in range(2):
            place = (slice(d + e, d + e + 3), slice(first, first + count))
            high = field_h[place].reshape(3 * count * chans, width)
            low = field_l[place].reshape(3 * count * chans, width)
            columns.append(jnp.concatenate([high, high, low], axis=0))
        return jnp.concatenate(columns, axis=1)

    dot = functools.partial(jnp.dot, preferred_element_type=F32)
    narrow(slice(1, depth + 1), slice(1, height + 1))
    arrive(first, True, range(0, 2))
    for d in (0, depth + 1):
        narrow(slice(d, d + 1), slice(1, height + 1))
    for block in range(blocks):
        for k in range(d2):
            partial[block, k] = dot(inner[block], across(2 * block + within[block][0], len(within[block]), 2 * k))
    arrive(first, True, range(2, len(WAYS)))
    for h in (0, height + 1):
        narrow(slice(0, depth + 2), slice(h, h + 1))
    halves = []
    for block in range(blocks):
        n, extra_hb, _ = beyond[block]
        for k in range(d2):
            extra = dot(outer[block], across(2 * block + n, 1, 2 * k))
            row = []
            for e in range(2):
                ends = []
                for hb in range(2):
                    x = partial[block, k, hb * 3 * chans : (hb + 1) * 3 * chans, e * width : (e + 1) * width]
                    if hb == extra_hb:
                        x = x + extra[:, e * width : (e + 1) * width]
                    ends.append(apart(x, width, chans))
                spot = (block * d2 + k) * 2 + e
                turned[spot] = gelu(jnp.concatenate(ends, axis=0)).T
                row += [turned[spot, pl.ds(c, half, stride=2), :] for c in range(2)]
            halves.append(jnp.concatenate(row, axis=1))
    lhs = jnp.concatenate(halves, axis=0)
    wide = dot(stacked(lhs), down1_w[...])
    cells1 = lhs.shape[0]
    total = wide[:cells1, :c2] + wide[:cells1, c2:] + wide[cells1:, :c2]
    total = total.reshape(h2, d2, half, c2)
    for h in range(h2):
        second[1 : d2 + 1, 1 + h] = total[h]
    again = halo(second, 1, second, send2, recv2)
    hand_on([[c] for c in spread], crossed, fourth, xsend, xrecv, crossings)

    def widen(h):
        @pl.loop(0, d2 + 2)
        def _(d):
            x = second[d, h]
            before, after = beside(x, half)
            spot = slice(h * 3 * c2, (h + 1) * 3 * c2)
            rows2[0, d, :, spot], rows2[1, d, :, spot] = split(jnp.concatenate([before, x, after], axis=1))

    def middle_term(a, low, high, left, right):
        lhs = rows2[:, a : a + d2, :, low:high].reshape(2 * d2 * half, high - low)
        return product(lhs, (middle_h[a, low:high, left:right], middle_l[a, low:high, left:right]))

    k3 = 3 * c2
    arrive(again, True, range(0, 2))
    for h in range(1, h2 + 1):
        widen(h)
    total, sides = None, [None, None]
    for a in range(3):
        total = plus(total, middle_term(a, k3, 3 * k3, 0, 2 * c2))
    arrive(again, True, range(2, len(WAYS)))
    for h in (0, h2 + 1):
        widen(h)
    for a in range(3):
        sides[0] = plus(sides[0], middle_term(a, 0, k3, 0, c2))
        sides[1] = plus(sides[1], middle_term(a, 3 * k3, 4 * k3, c2, 2 * c2))
    hand_on(crossed, forward, half_taps, fsend, frecv, [sibling])
    for h in range(h2):
        level2[h] = gelu(total[:, h * c2 : (h + 1) * c2] + sides[h])
    quarter = half // 2
    lhs = jnp.concatenate(
        [
            level2[h, pl.ds(d * half + c, quarter, stride=2), :]
            for d in range(d2) for h in range(h2) for c in range(2)
        ],
        axis=1,
    )
    lhs = stacked(lhs)
    for made in forward:
        made[0].wait_recv()
    weights = jnp.concatenate(
        [gathered[:, t].reshape(groups * shard.shape[1], c2) for t in range(taps_of)], axis=1
    )
    share = product(lhs, split(weights), (((1,), (1,)), ((), ())))
    coarse[pl.ds(g, 1)] = share[None]
    sent = []
    for j in range(1, groups):
        copy = pltpu.make_async_remote_copy(
            src_ref=coarse.at[g],
            dst_ref=coarse.at[g],
            send_sem=csend.at[j],
            recv_sem=crecv.at[j],
            device_id=(s, lax.rem(g + j, groups)),
            device_id_type=MESH,
        )
        copy.start()
        sent.append(copy)
    cells = groups * quarter
    edge = jnp.zeros((2, quarter, taps.shape[2]), BF16)
    taps[:, 0:quarter] = edge
    taps[:, quarter + cells : 2 * quarter + cells] = edge
    for copy in sent:
        copy.wait_recv()
    x = coarse[...].reshape(cells, coarse.shape[2])
    before, after = beside(x, quarter)
    taps[0, quarter : quarter + cells], taps[1, quarter : quarter + cells] = split(
        jnp.concatenate([before, x, after], axis=1)
    )

    def plane(high, low):
        total = None
        for b in range(3):
            lhs = taps[:, b * quarter : b * quarter + cells].reshape(2 * cells, taps.shape[2])
            total = plus(total, product(lhs, (high[b], low[b])))
        return total

    both = plane(edges_h, edges_l)
    upward[...] = both[:, :outs]
    downward[...] = both[:, outs:]
    up = pltpu.make_async_remote_copy(
        src_ref=upward, dst_ref=from_lower, send_sem=psend.at[0], recv_sem=precv.at[0],
        device_id=(s + 1, g), device_id_type=MESH,
    )
    down = pltpu.make_async_remote_copy(
        src_ref=downward, dst_ref=from_upper, send_sem=psend.at[1], recv_sem=precv.at[1],
        device_id=(s - 1, g), device_id_type=MESH,
    )

    @pl.when(exists(1, 0))
    def _():
        up.start()

    @pl.when(jnp.logical_not(exists(-1, 0)))
    def _():
        from_lower[...] = jnp.zeros(from_lower.shape, F32)

    @pl.when(exists(-1, 0))
    def _():
        down.start()

    @pl.when(jnp.logical_not(exists(1, 0)))
    def _():
        from_upper[...] = jnp.zeros(from_upper.shape, F32)

    centre = plane(centre_h, centre_l)

    @pl.when(exists(-1, 0))
    def _():
        up.wait_recv()

    @pl.when(exists(1, 0))
    def _():
        down.wait_recv()

    out[...] = gelu(centre + from_lower[...] + from_upper[...]).T

    arrive(first, False)
    arrive(again, False)
    for copy in spread + sum(crossed + forward, []) + sent:
        copy.wait_send()

    @pl.when(exists(1, 0))
    def _():
        up.wait_send()

    @pl.when(exists(-1, 0))
    def _():
        down.wait_send()


def per_device(slabs, groups, volume, conv_fine, down_first, conv_middle, down_second, conv_coarse):
    c1, depth, height, width = volume.shape
    c2, c3, c4 = down_first.shape[4], conv_coarse.shape[3], conv_coarse.shape[4]
    half, quarter = width // 2, width // 4
    d2, h2 = depth // 2, height // 2
    part = down_second.shape[4]
    cells = groups * quarter
    vol = volume.reshape(c1 * depth * height, width)
    fine = conv_fine.reshape(27, c1, c1)
    down1 = down_first.reshape(2, 4 * c1, c2)
    middle = conv_middle.reshape(9, 3 * c2, c2)
    shard = jnp.swapaxes(down_second, 3, 4).reshape(8, part, c2)
    coarse_w = conv_coarse.reshape(9, 3 * c3, c4)
    V = pltpu.VMEM
    vmem, away = pl.BlockSpec(memory_space=pltpu.VMEM), pl.BlockSpec(memory_space=pl.ANY)
    dma = pltpu.SemaphoreType.DMA
    result = pl.pallas_call(
        functools.partial(kernel, slabs, groups),
        out_shape=pltpu.VMEM((c4, cells), F32),
        in_specs=[away] * 6,
        out_specs=vmem,
        scratch_shapes=[
            V(vol.shape, F32),
            V(fine.shape, F32),
            V((depth + 2, height + 2, c1, width), F32),
            V((depth + 2, height + 2, c1, width), BF16),
            V((depth + 2, height + 2, c1, width), BF16),
            V((2, 6 * c1, 27 * c1), BF16),
            V((2, 3 * c1, 9 * c1), BF16),
            V((2, d2, 6 * c1, 2 * width), F32),
            V((2 * d2 * 2, width, 2 * c1), F32),
            V(down1.shape, F32),
            V((8 * c1, 2 * c2), BF16),
            V(middle.shape, F32),
            V((3, 12 * c2, 2 * c2), BF16),
            V((3, 12 * c2, 2 * c2), BF16),
            V((d2 + 2, h2 + 2, half, c2), F32),
            V((2, d2 + 2, half, 12 * c2), BF16),
            V((h2, d2 * half, c2), F32),
            V((groups,) + shard.shape, F32),
            V(coarse_w.shape, F32),
            V((3, 3 * c3, 2 * c4), BF16),
            V((3, 3 * c3, 2 * c4), BF16),
            V((3, 3 * c3, c4), BF16),
            V((3, 3 * c3, c4), BF16),
            V((groups, quarter, c3), F32),
            V((2, cells + 2 * quarter, 3 * c3), BF16),
            V((cells, c4), F32),
            V((cells, c4), F32),
            V((cells, c4), F32),
            V((cells, c4), F32),
            dma((6,)),
            dma((8,)), dma((8,)), dma((8,)), dma((8,)),
            dma((groups,)), dma((groups,)), dma((groups, 3)), dma((groups, 3)), dma((groups, 1)), dma((groups, 1)), dma((groups,)), dma((groups,)),
            dma((2,)), dma((2,)),
        ],
        compiler_params=pltpu.CompilerParams(
            collective_id=0, has_side_effects=True, vmem_limit_bytes=60 * 1024 * 1024
        ),
    )(vol, fine, down1, middle, shard, coarse_w)
    return result.reshape(c4, 1, cells)


def solution(mesh):
    placed = (
        P(None, "slab", "grp", None),
        P(),
        P(),
        P(),
        P(None, None, None, None, "grp"),
        P(None, None, None, None, "grp"),
    )
    body = functools.partial(per_device, mesh.shape["slab"], mesh.shape["grp"])
    return jax.shard_map(
        body, mesh=mesh, in_specs=placed, out_specs=P("grp", "slab", None), check_vma=False
    )
```

```python
import functools

import jax
import jax.numpy as jnp
from jax import lax
from jax.experimental import pallas as pl
from jax.experimental.pallas import tpu as pltpu
from jax.sharding import PartitionSpec as P

MESH = pl.DeviceIdType.MESH
F32, BF16 = jnp.float32, jnp.bfloat16
WAYS = ((1, 0), (-1, 0), (0, 1), (0, -1), (1, 1), (1, -1), (-1, 1), (-1, -1))


def split(x):
    high = x.astype(BF16)
    return high, (x - high.astype(F32)).astype(BF16)


def stacked(x):
    return jnp.concatenate(split(x), axis=0)


def product(both, weights, dims=(((1,), (0,)), ((), ()))):
    dot = functools.partial(lax.dot_general, dimension_numbers=dims, preferred_element_type=F32)
    rows = both.shape[0] // 2
    wide = dot(both, weights[0])
    return wide[:rows] + wide[rows:] + dot(both[:rows], weights[1])


def plus(total, term):
    return term if total is None else total + term


def gelu(x):
    return 0.5 * x * (1.0 + lax.erf(x * (0.5**0.5)))


def apart(x, width, chans):
    lane = lax.broadcasted_iota(jnp.int32, (chans, width), 1)
    before = jnp.where(lane == 0, 0.0, pltpu.roll(x[:chans], 1, 1))
    after = jnp.where(lane == width - 1, 0.0, pltpu.roll(x[2 * chans :], width - 1, 1))
    return before + x[chans : 2 * chans] + after


def beside(x, span):
    at = lax.rem(lax.broadcasted_iota(jnp.int32, x.shape, 0), span)
    before = jnp.where(at == 0, 0.0, pltpu.roll(x, 1, 0))
    after = jnp.where(at == span - 1, 0.0, pltpu.roll(x, x.shape[0] - 1, 0))
    return before, after


def kernel(
    slabs, groups,
    vol_hbm, fine_hbm, down1_hbm, middle_hbm, shard, coarse_hbm,
    out,
    vol, fine, field, field_h, field_l, inner, outer, partial, turned, down1, down1_w, middle,
    mid_h, mid_l, side_h, side_l, second, second_h, second_l, level2, gathered, coarse_w, coarse_b,
    coarse, sums,
    load_sem, send1, recv1, send2, recv2, wsend, wrecv, xsend, xrecv, fsend, frecv, csend, crecv, nsend, nrecv,
):
    s, g = lax.axis_index("slab"), lax.axis_index("grp")
    depth, height, chans, width = (field.shape[0] - 2, field.shape[1] - 2) + field.shape[2:]
    half = width // 2

    loads = [
        pltpu.make_async_copy(vol_hbm, vol, load_sem.at[3]),
        pltpu.make_async_copy(fine_hbm, fine, load_sem.at[4]),
        pltpu.make_async_copy(shard, gathered.at[g], load_sem.at[5]),
        pltpu.make_async_copy(down1_hbm, down1, load_sem.at[0]),
        pltpu.make_async_copy(middle_hbm, middle, load_sem.at[1]),
        pltpu.make_async_copy(coarse_hbm, coarse_w, load_sem.at[2]),
    ]
    for load in loads:
        load.start()

    def exists(ds, dg):
        return (s + ds >= 0) & (s + ds < slabs) & (g + dg >= 0) & (g + dg < groups)

    barrier = pltpu.get_barrier_semaphore()
    heard = jnp.int32(0)
    for ds, dg in WAYS:
        there = exists(ds, dg)
        heard = heard + there.astype(jnp.int32)

        @pl.when(there)
        def _():
            pl.semaphore_signal(barrier, inc=1, device_id=(s + ds, g + dg), device_id_type=MESH)

    for dg in range(2, groups):
        for sign in (1, -1):
            there = exists(0, sign * dg)
            heard = heard + there.astype(jnp.int32)

            @pl.when(there)
            def _():
                pl.semaphore_signal(barrier, inc=1, device_id=(s, g + sign * dg), device_id_type=MESH)

    sibling = s + 1 - 2 * lax.rem(s, 2)
    low, high = lax.rem(s // 2, 2), lax.rem(s // 4, 2)
    crossings = [s + 2 - 4 * low, s + 4 - 8 * high, s + 6 - 4 * low - 8 * high]
    for peer in crossings:
        pl.semaphore_signal(barrier, inc=1, device_id=(peer, g), device_id_type=MESH)
    pl.semaphore_wait(barrier, heard + len(crossings))

    taps_of = shard.shape[0]
    parity = lax.rem(s, 2)
    eighth = pl.ds((parity * 4 + lax.rem(s // 2, 4)) * (taps_of // 8), taps_of // 8)
    half_taps = pl.ds(parity * (taps_of // 2), taps_of // 2)
    spread, crossed, forward = [], [], []
    for j in range(1, groups):
        copy = pltpu.make_async_remote_copy(
            src_ref=shard.at[eighth],
            dst_ref=gathered.at[g, eighth],
            send_sem=wsend.at[j],
            recv_sem=wrecv.at[j],
            device_id=(s, lax.rem(g + j, groups)),
            device_id_type=MESH,
        )
        copy.start()
        spread.append(copy)

    loads[0].wait()
    lines = depth * height
    for r in range(lines):
        field[1 + r // height, 1 + r % height] = vol[pl.ds(r, chans, stride=lines), :]
    def part(way, size, offset):
        if way == 0:
            return pl.ds(offset, size)
        return pl.ds(offset + (size - 1 if way > 0 else 0), 1)

    def landing(way, size):
        if way == 0:
            return pl.ds(1, size)
        return pl.ds(0 if way > 0 else size + 1, 1)

    def halo(src, offset, buf, sends, recvs):
        nd, nh = buf.shape[0] - 2, buf.shape[1] - 2
        copies = []
        for k, (ds, dg) in enumerate(WAYS):
            copies.append(
                pltpu.make_async_remote_copy(
                    src_ref=src.at[part(ds, nd, offset), part(dg, nh, offset)],
                    dst_ref=buf.at[landing(ds, nd), landing(dg, nh)],
                    send_sem=sends.at[k],
                    recv_sem=recvs.at[k],
                    device_id=(s + ds, g + dg),
                    device_id_type=MESH,
                )
            )

            @pl.when(exists(ds, dg))
            def _():
                copies[k].start()

            @pl.when(jnp.logical_not(exists(-ds, -dg)))
            def _():
                piece = (landing(ds, nd), landing(dg, nh))
                shape = (piece[0].size, piece[1].size) + buf.shape[2:]
                buf[piece[0], piece[1]] = jnp.zeros(shape, F32)

        return copies

    def arrive(copies, received, ways=range(len(WAYS))):
        for k in ways:
            ds, dg = WAYS[k]
            if received:
                @pl.when(exists(-ds, -dg))
                def _():
                    copies[k].wait_recv()
            else:
                @pl.when(exists(ds, dg))
                def _():
                    copies[k].wait_send()

    first = halo(field, 1, field, send1, recv1)

    def hand_on(arrived, out_copies, piece, sends, recvs, peers):
        for j in range(1, groups):
            for copy in arrived[j - 1]:
                copy.wait_recv()
            source = lax.rem(g + groups - j, groups)
            made = []
            for k, peer in enumerate(peers):
                copy = pltpu.make_async_remote_copy(
                    src_ref=gathered.at[source, piece],
                    dst_ref=gathered.at[source, piece],
                    send_sem=sends.at[j, k],
                    recv_sem=recvs.at[j, k],
                    device_id=(peer, g),
                    device_id_type=MESH,
                )
                copy.start()
                made.append(copy)
            out_copies.append(made)

    loads[1].wait()
    blocks = height // 2
    blank = jnp.zeros((3 * chans, chans), BF16)
    wide = jnp.concatenate(
        [
            jnp.concatenate([fine[ab * 3 + c] for c in range(3)], axis=1)
            for ab in range(9)
        ],
        axis=0,
    )
    both = split(wide.T)

    def taps_at(x, b):
        return [x[:, (a * 3 + b) * chans : (a * 3 + b + 1) * chans] for a in range(3)] if 0 <= b < 3 else [blank] * 3

    within = [[n for n in range(4) if 1 <= 2 * block + n <= height] for block in range(blocks)]
    beyond = [(0, 0, 0), (3, 1, 2)]
    for block in range(blocks):
        for hb in range(2):
            parts = []
            for x in both:
                by_line = [taps_at(x, n - hb) for n in within[block]]
                parts.append(jnp.concatenate([line[a] for a in range(3) for line in by_line], axis=1))
            inner[block, hb * 3 * chans : (hb + 1) * 3 * chans] = jnp.concatenate([parts[0], parts[1], parts[0]], axis=1)
    for k, (_, _, b) in enumerate(beyond):
        parts = [jnp.concatenate(taps_at(x, b), axis=1) for x in both]
        outer[k] = jnp.concatenate([parts[0], parts[1], parts[0]], axis=1)
    d2, h2, c2 = depth // 2, blocks, down1.shape[2]
    for load in loads[2:5]:
        load.wait()
    for a in range(2):
        for b in range(2):
            for c in range(2):
                spot = pl.ds(((a * 2 + c) * 2 + b) * chans, chans)
                down1_w[spot, 0:c2], down1_w[spot, c2 : 2 * c2] = split(down1[a, (b * 2 + c) * chans : (b * 2 + c + 1) * chans])

    @pl.loop(0, 3)
    def _(a):
        for line in range(1, h2 + 1):
            rows = pl.ds(pl.multiple_of((a * h2 + line - 1) * c2, c2), c2)
            for hb in range(h2):
                for c in range(3):
                    columns = pl.ds((hb * 3 + c) * c2, c2)
                    if 0 <= line - hb < 3:
                        mid_h[rows, columns], mid_l[rows, columns] = split(middle[a * 3 + line - hb, c * c2 : (c + 1) * c2])
                    else:
                        mid_h[rows, columns] = mid_l[rows, columns] = jnp.zeros((c2, c2), BF16)
        rows = pl.ds(pl.multiple_of(a * c2, c2), c2)
        for k, b in ((0, 0), (1, 2)):
            for c in range(3):
                columns = pl.ds(c * c2, c2)
                side_h[k, rows, columns], side_l[k, rows, columns] = split(middle[a * 3 + b, c * c2 : (c + 1) * c2])

    outs = coarse_w.shape[2]
    c3 = coarse.shape[3]

    def prepare_coarse():
        loads[5].wait()

        @pl.loop(0, 3)
        def _(a):
            for b in range(3):
                for c in range(3):
                    high, low = split(coarse_w[a * 3 + b, c * c3 : (c + 1) * c3])
                    spot = (b * 3 + c) * outs
                    coarse_b[a, :, spot : spot + outs] = high
                    coarse_b[a, :, 9 * outs + spot : 10 * outs + spot] = low

    def narrow(ds, hs):
        field_h[ds, hs], field_l[ds, hs] = split(field[ds, hs])

    def across(first, count, d):
        columns = []
        for e in range(2):
            place = (pl.ds(d + e, 3), slice(first, first + count))
            high = field_h[place].reshape(3 * count * chans, width)
            low = field_l[place].reshape(3 * count * chans, width)
            columns.append(jnp.concatenate([high, high, low], axis=0))
        return jnp.concatenate(columns, axis=1)

    dot = functools.partial(jnp.dot, preferred_element_type=F32)
    narrow(slice(1, depth + 1), slice(1, height + 1))
    pairs = [jnp.where(parity == 0, d2 - 1, 0)] + list(range(1, d2 - 1))
    pairs.append(d2 - 1 - pairs[0])
    for n, k in enumerate(pairs):
        if n in (0, d2 - 1):
            for way in range(2):
                mine = (parity == 1 - way) if n == 0 else (parity == way)

                @pl.when(mine)
                def _():
                    arrive(first, True, (way,))
            narrow(pl.ds(jnp.where(k == 0, 0, depth + 1), 1), slice(1, height + 1))
        for block in range(blocks):
            partial[block, k] = dot(inner[block], across(2 * block + within[block][0], len(within[block]), 2 * k))
    hand_on([[c] for c in spread], crossed, eighth, xsend, xrecv, crossings)
    arrive(first, True, range(2, len(WAYS)))
    for h in (0, height + 1):
        narrow(slice(0, depth + 2), slice(h, h + 1))
    halves = []
    for block in range(blocks):
        n, extra_hb, _ = beyond[block]
        for k in range(d2):
            extra = dot(outer[block], across(2 * block + n, 1, 2 * k))
            row = []
            for e in range(2):
                ends = []
                for hb in range(2):
                    x = partial[block, k, hb * 3 * chans : (hb + 1) * 3 * chans, e * width : (e + 1) * width]
                    if hb == extra_hb:
                        x = x + extra[:, e * width : (e + 1) * width]
                    ends.append(apart(x, width, chans))
                spot = (block * d2 + k) * 2 + e
                turned[spot] = gelu(jnp.concatenate(ends, axis=0)).T
                row += [turned[spot, pl.ds(c, half, stride=2), :] for c in range(2)]
            halves.append(jnp.concatenate(row, axis=1))
    lhs = jnp.concatenate(halves, axis=0)
    wide = dot(stacked(lhs), down1_w[...])
    cells1 = lhs.shape[0]
    total = wide[:cells1, :c2] + wide[:cells1, c2:] + wide[cells1:, :c2]
    total = total.reshape(h2, d2, half, c2)
    for h in range(h2):
        second[1 : d2 + 1, 1 + h] = total[h]
    again = halo(second, 1, second, send2, recv2)
    prepare_coarse()
    def thin(h):
        spot = slice(h * c2, (h + 1) * c2)
        second_h[:, :, spot], second_l[:, :, spot] = split(second[:, h])

    def gathered_taps(low, high):
        parts = []
        for x in (second_h, second_l):
            parts.append(
                jnp.concatenate([x[a : a + d2, :, low:high].reshape(d2 * half, high - low) for a in range(3)], axis=1)
            )
        return jnp.concatenate(parts, axis=0)

    arrive(again, True, range(0, 2))
    for h in range(1, h2 + 1):
        thin(h)
    total = product(gathered_taps(c2, (1 + h2) * c2), (mid_h[...], mid_l[...]))
    hand_on(crossed, forward, half_taps, fsend, frecv, [sibling])
    arrive(again, True, range(2, len(WAYS)))
    for h in (0, h2 + 1):
        thin(h)
    sides = [
        product(gathered_taps(h * c2, (h + 1) * c2), (side_h[k], side_l[k])) for k, h in ((0, 0), (1, h2 + 1))
    ]
    for h in range(h2):
        x = total[:, h * 3 * c2 : (h + 1) * 3 * c2]
        if h == 0:
            x = x + sides[0]
        if h == h2 - 1:
            x = x + sides[1]
        before, _ = beside(x[:, :c2], half)
        _, after = beside(x[:, 2 * c2 :], half)
        level2[h] = gelu(before + x[:, c2 : 2 * c2] + after)
    quarter = half // 2
    lhs = jnp.concatenate(
        [
            level2[h, pl.ds(d * half + c, quarter, stride=2), :]
            for d in range(d2) for h in range(h2) for c in range(2)
        ],
        axis=1,
    )
    lhs = stacked(lhs)
    for made in forward:
        made[0].wait_recv()
    weights = jnp.concatenate(
        [gathered[:, t].reshape(groups * shard.shape[1], c2) for t in range(taps_of)], axis=1
    )
    share = product(lhs, split(weights), (((1,), (1,)), ((), ())))
    coarse[1, pl.ds(g, 1)] = share[None]
    cells = groups * quarter

    def nth(n):
        spare = jnp.minimum(g, groups - 1 - g)
        near = (n + 1) // 2 if n % 2 else -(n // 2)
        away = jnp.where(2 * g < groups - 1, 1, -1)
        return g + jnp.where(n <= 2 * spare, near, away * (n - spare))

    sent = []

    def send(there, line, plane, peer, sends, recvs):
        copy = pltpu.make_async_remote_copy(
            src_ref=coarse.at[1, line], dst_ref=coarse.at[plane, line], send_sem=sends, recv_sem=recvs,
            device_id=peer, device_id_type=MESH,
        )

        @pl.when(there)
        def _():
            copy.start()

        sent.append((there, copy))

    order = [nth(n) for n in range(groups)]

    def sideways(n):
        for k, ds in enumerate((1, -1)):
            send(exists(ds, 0), order[n], 1 - ds, (s + ds, g), nsend.at[k, n], nrecv.at[1 - ds, order[n]])

    for k, dg in enumerate(d for d in range(1 - groups, groups) if d):
        send(exists(0, dg), g, 1, (s, g + dg), csend.at[k], crecv.at[g])
    sideways(0)

    def landed(n, plane):
        line = order[n]
        sems = crecv.at[line] if plane == 1 else nrecv.at[plane, line]
        copy = pltpu.make_async_remote_copy(
            src_ref=coarse.at[plane, line], dst_ref=coarse.at[plane, line], send_sem=csend.at[0], recv_sem=sems,
            device_id=(s, g), device_id_type=MESH,
        )
        if plane == 1:
            copy.wait_recv()
        else:
            @pl.when(exists(plane - 1, 0))
            def _():
                copy.wait_recv()

    def terms(ns, plane):
        x = jnp.concatenate([coarse[plane, pl.ds(order[n], 1)][0] for n in ns], axis=0)
        size = len(ns) * quarter
        wide = dot(stacked(x), coarse_b[plane])
        span = 9 * outs
        wide = wide[:size, :span] + wide[:size, span:] + wide[size:, :span]
        for k, n in enumerate(ns):
            for b in range(3):
                spot = pl.ds(pl.multiple_of((order[n] + 2 - b) * quarter, quarter), quarter)
                sums[spot] = sums[spot] + wide[k * quarter : (k + 1) * quarter, b * 3 * outs : (b + 1) * 3 * outs]

    def own(ns):
        for n in ns:
            if n:
                landed(n, 1)
                sideways(n)
        terms(ns, 1)

    def others(ns):
        for plane in (0, 2):
            for n in ns:
                landed(n, plane)
        for plane in (0, 2):
            terms(ns, plane)

    for plane in (0, 2):
        @pl.when(jnp.logical_not(exists(plane - 1, 0)))
        def _():
            coarse[plane] = jnp.zeros(coarse.shape[1:], F32)

    sums[...] = jnp.zeros(sums.shape, F32)
    stages = [[0]] + [list(range(n, min(n + 2, groups))) for n in range(1, groups, 2)]
    for k, stage in enumerate(stages):
        own(stage)
        if 0 < k < len(stages) - 1:
            others(stages[k - 1])
    for stage in stages[-2:]:
        others(stage)
    x = sums[quarter : quarter + cells]
    before, _ = beside(x[:, :outs], quarter)
    _, after = beside(x[:, 2 * outs :], quarter)
    out[...] = gelu(before + x[:, outs : 2 * outs] + after).T

    arrive(first, False)
    arrive(again, False)
    for copy in spread + sum(crossed + forward, []):
        copy.wait_send()
    for there, copy in sent:
        @pl.when(there)
        def _():
            copy.wait_send()


def per_device(slabs, groups, volume, conv_fine, down_first, conv_middle, down_second, conv_coarse):
    c1, depth, height, width = volume.shape
    c2, c3, c4 = down_first.shape[4], conv_coarse.shape[3], conv_coarse.shape[4]
    half, quarter = width // 2, width // 4
    d2, h2 = depth // 2, height // 2
    part = down_second.shape[4]
    cells = groups * quarter
    vol = volume.reshape(c1 * depth * height, width)
    fine = conv_fine.reshape(27, c1, c1)
    down1 = down_first.reshape(2, 4 * c1, c2)
    middle = conv_middle.reshape(9, 3 * c2, c2)
    shard = jnp.swapaxes(down_second, 3, 4).reshape(8, part, c2)
    coarse_w = conv_coarse.reshape(9, 3 * c3, c4)
    V = pltpu.VMEM
    vmem, away = pl.BlockSpec(memory_space=pltpu.VMEM), pl.BlockSpec(memory_space=pl.ANY)
    dma = pltpu.SemaphoreType.DMA
    result = pl.pallas_call(
        functools.partial(kernel, slabs, groups),
        out_shape=pltpu.VMEM((c4, cells), F32),
        in_specs=[away] * 6,
        out_specs=vmem,
        scratch_shapes=[
            V(vol.shape, F32),
            V(fine.shape, F32),
            V((depth + 2, height + 2, c1, width), F32),
            V((depth + 2, height + 2, c1, width), BF16),
            V((depth + 2, height + 2, c1, width), BF16),
            V((2, 6 * c1, 27 * c1), BF16),
            V((2, 3 * c1, 9 * c1), BF16),
            V((2, d2, 6 * c1, 2 * width), F32),
            V((2 * d2 * 2, width, 2 * c1), F32),
            V(down1.shape, F32),
            V((8 * c1, 2 * c2), BF16),
            V(middle.shape, F32),
            V((3 * h2 * c2, 3 * h2 * c2), BF16),
            V((3 * h2 * c2, 3 * h2 * c2), BF16),
            V((2, 3 * c2, 3 * c2), BF16),
            V((2, 3 * c2, 3 * c2), BF16),
            V((d2 + 2, h2 + 2, half, c2), F32),
            V((d2 + 2, half, (h2 + 2) * c2), BF16),
            V((d2 + 2, half, (h2 + 2) * c2), BF16),
            V((h2, d2 * half, c2), F32),
            V((groups,) + shard.shape, F32),
            V(coarse_w.shape, F32),
            V((3, c3, 18 * c4), BF16),
            V((3, groups, quarter, c3), F32),
            V((cells + 2 * quarter, 3 * c4), F32),
            dma((6,)),
            dma((8,)), dma((8,)), dma((8,)), dma((8,)),
            dma((groups,)), dma((groups,)), dma((groups, 3)), dma((groups, 3)), dma((groups, 1)), dma((groups, 1)), dma((2 * groups,)), dma((groups,)),
            dma((2, groups)), dma((3, groups)),
        ],
        compiler_params=pltpu.CompilerParams(
            collective_id=0, has_side_effects=True, vmem_limit_bytes=60 * 1024 * 1024
        ),
    )(vol, fine, down1, middle, shard, coarse_w)
    return result.reshape(c4, 1, cells)


def solution(mesh):
    placed = (
        P(None, "slab", "grp", None),
        P(),
        P(),
        P(),
        P(None, None, None, None, "grp"),
        P(None, None, None, None, "grp"),
    )
    body = functools.partial(per_device, mesh.shape["slab"], mesh.shape["grp"])
    return jax.shard_map(
        body, mesh=mesh, in_specs=placed, out_specs=P("grp", "slab", None), check_vma=False
    )
```

```python
import functools

import jax
import jax.numpy as jnp
from jax import lax
from jax.experimental import pallas as pl
from jax.experimental.pallas import tpu as pltpu
from jax.sharding import PartitionSpec as P

MESH = pl.DeviceIdType.MESH
F32, BF16 = jnp.float32, jnp.bfloat16
WAYS = ((1, 0), (-1, 0), (0, 1), (0, -1), (1, 1), (1, -1), (-1, 1), (-1, -1))


def split(x):
    high = x.astype(BF16)
    return high, (x - high.astype(F32)).astype(BF16)


def stacked(x):
    return jnp.concatenate(split(x), axis=0)


def product(both, weights, dims=(((1,), (0,)), ((), ()))):
    dot = functools.partial(lax.dot_general, dimension_numbers=dims, preferred_element_type=F32)
    rows = both.shape[0] // 2
    wide = dot(both, weights[0])
    return wide[:rows] + wide[rows:] + dot(both[:rows], weights[1])


def plus(total, term):
    return term if total is None else total + term


def gelu(x):
    return 0.5 * x * (1.0 + lax.erf(x * (0.5**0.5)))


def apart(x, width, chans):
    lane = lax.broadcasted_iota(jnp.int32, (chans, width), 1)
    before = jnp.where(lane == 0, 0.0, pltpu.roll(x[:chans], 1, 1))
    after = jnp.where(lane == width - 1, 0.0, pltpu.roll(x[2 * chans :], width - 1, 1))
    return before + x[chans : 2 * chans] + after


def beside(x, span):
    at = lax.rem(lax.broadcasted_iota(jnp.int32, x.shape, 0), span)
    before = jnp.where(at == 0, 0.0, pltpu.roll(x, 1, 0))
    after = jnp.where(at == span - 1, 0.0, pltpu.roll(x, x.shape[0] - 1, 0))
    return before, after


def kernel(
    slabs, groups,
    vol_hbm, fine_hbm, down1_hbm, middle_hbm, shard, coarse_hbm,
    out,
    vol, fine, field, field_h, field_l, inner, outer, partial, turned, down1, down1_w, middle,
    mid_h, mid_l, side_h, side_l, second, second_h, second_l, level2, gathered, coarse_w, coarse_b,
    coarse, sums,
    load_sem, ready, send1, recv1, send2, recv2, wsend, wrecv, xsend, xrecv, fsend, frecv, csend, crecv, nsend, nrecv,
):
    s, g = lax.axis_index("slab"), lax.axis_index("grp")
    depth, height, chans, width = (field.shape[0] - 2, field.shape[1] - 2) + field.shape[2:]
    half = width // 2

    loads = [
        pltpu.make_async_copy(vol_hbm, vol, load_sem.at[3]),
        pltpu.make_async_copy(fine_hbm, fine, load_sem.at[4]),
        pltpu.make_async_copy(shard, gathered.at[g], load_sem.at[5]),
        pltpu.make_async_copy(down1_hbm, down1, load_sem.at[0]),
        pltpu.make_async_copy(middle_hbm, middle, load_sem.at[1]),
        pltpu.make_async_copy(coarse_hbm, coarse_w, load_sem.at[2]),
    ]
    for load in loads:
        load.start()

    def exists(ds, dg):
        return (s + ds >= 0) & (s + ds < slabs) & (g + dg >= 0) & (g + dg < groups)

    barrier = pltpu.get_barrier_semaphore()
    heard = jnp.int32(0)
    for ds, dg in WAYS[:4]:
        there = exists(ds, dg)
        heard = heard + there.astype(jnp.int32)

        @pl.when(there)
        def _():
            pl.semaphore_signal(barrier, inc=1, device_id=(s + ds, g + dg), device_id_type=MESH)

    sibling = s + 1 - 2 * lax.rem(s, 2)
    low, high = lax.rem(s // 2, 2), lax.rem(s // 4, 2)
    crossings = [s + 2 - 4 * low, s + 4 - 8 * high, s + 6 - 4 * low - 8 * high]
    for peer in crossings:
        pl.semaphore_signal(barrier, inc=1, device_id=(peer, g), device_id_type=MESH)
    pl.semaphore_wait(barrier, heard + len(crossings))

    taps_of = shard.shape[0]
    parity = lax.rem(s, 2)
    eighth = pl.ds((parity * 4 + lax.rem(s // 2, 4)) * (taps_of // 8), taps_of // 8)
    half_taps = pl.ds(parity * (taps_of // 2), taps_of // 2)
    def nth(n):
        spare = jnp.minimum(g, groups - 1 - g)
        near = (n + 1) // 2 if n % 2 else -(n // 2)
        away = jnp.where(2 * g < groups - 1, 1, -1)
        return g + jnp.where(n <= 2 * spare, near, away * (n - spare))

    order = [nth(n) for n in range(groups)]
    spread, crossed, forward = [], [], []
    rounds = max(1, groups - 2)

    def spread_to(dg):
        copy = pltpu.make_async_remote_copy(
            src_ref=shard.at[eighth], dst_ref=gathered.at[g, eighth],
            send_sem=wsend.at[dg + groups - 1], recv_sem=wrecv.at[g],
            device_id=(s, g + dg), device_id_type=MESH,
        )

        @pl.when(exists(0, dg))
        def _():
            copy.start()

        spread.append((exists(0, dg), copy))

    def announce(n):
        for ds, dg in WAYS[:4] if n == 0 else WAYS[2:4]:
            @pl.when(exists(ds, dg))
            def _():
                pl.semaphore_signal(ready.at[n], inc=1, device_id=(s + ds, g + dg), device_id_type=MESH)

    def listen(n):
        count = jnp.int32(0)
        for ds, dg in WAYS[:4] if n == 0 else WAYS[2:4]:
            count = count + exists(ds, dg).astype(jnp.int32)
        pl.semaphore_wait(ready.at[n], count)

    announce(0)
    for dg in (1, -1):
        spread_to(dg)

    loads[0].wait()
    lines = depth * height
    for r in range(lines):
        field[1 + r // height, 1 + r % height] = vol[pl.ds(r, chans, stride=lines), :]
    def part(way, size, offset):
        if way == 0:
            return pl.ds(offset, size)
        return pl.ds(offset + (size - 1 if way > 0 else 0), 1)

    def landing(way, size):
        if way == 0:
            return pl.ds(1, size)
        return pl.ds(0 if way > 0 else size + 1, 1)

    def halo(src, offset, buf, sends, recvs, between=None):
        nd, nh = buf.shape[0] - 2, buf.shape[1] - 2
        copies = []
        for k, (ds, dg) in enumerate(WAYS):
            if k == 4 and between is not None:
                between()
            copies.append(
                pltpu.make_async_remote_copy(
                    src_ref=src.at[part(ds, nd, offset), part(dg, nh, offset)],
                    dst_ref=buf.at[landing(ds, nd), landing(dg, nh)],
                    send_sem=sends.at[k],
                    recv_sem=recvs.at[k],
                    device_id=(s + ds, g + dg),
                    device_id_type=MESH,
                )
            )

            @pl.when(exists(ds, dg))
            def _():
                copies[k].start()

            @pl.when(jnp.logical_not(exists(-ds, -dg)))
            def _():
                piece = (landing(ds, nd), landing(dg, nh))
                shape = (piece[0].size, piece[1].size) + buf.shape[2:]
                buf[piece[0], piece[1]] = jnp.zeros(shape, F32)

        return copies

    def arrive(copies, received, ways=range(len(WAYS))):
        for k in ways:
            ds, dg = WAYS[k]
            if received:
                @pl.when(exists(-ds, -dg))
                def _():
                    copies[k].wait_recv()
            else:
                @pl.when(exists(ds, dg))
                def _():
                    copies[k].wait_send()

    def further():
        for n in range(rounds):
            listen(n)
            if n + 1 < rounds:
                announce(n + 1)
            if n + 2 < groups:
                for dg in (n + 2, -n - 2):
                    spread_to(dg)

    first = halo(field, 1, field, send1, recv1, further)

    def hand_on(arrived, out_copies, piece, sends, recvs, peers):
        for n in range(1, groups):
            source = order[n]
            for copy in arrived(n, source):
                copy.wait_recv()
            made = []
            for k, peer in enumerate(peers):
                copy = pltpu.make_async_remote_copy(
                    src_ref=gathered.at[source, piece],
                    dst_ref=gathered.at[source, piece],
                    send_sem=sends.at[n, k],
                    recv_sem=recvs.at[n, k],
                    device_id=(peer, g),
                    device_id_type=MESH,
                )
                copy.start()
                made.append(copy)
            out_copies.append(made)

    def from_group(n, source):
        return [
            pltpu.make_async_remote_copy(
                src_ref=gathered.at[source, eighth], dst_ref=gathered.at[source, eighth],
                send_sem=wsend.at[0], recv_sem=wrecv.at[source], device_id=(s, g), device_id_type=MESH,
            )
        ]

    loads[1].wait()
    blocks = height // 2
    blank = jnp.zeros((3 * chans, chans), BF16)
    wide = jnp.concatenate(
        [
            jnp.concatenate([fine[ab * 3 + c] for c in range(3)], axis=1)
            for ab in range(9)
        ],
        axis=0,
    )
    both = split(wide.T)

    def taps_at(x, b):
        return [x[:, (a * 3 + b) * chans : (a * 3 + b + 1) * chans] for a in range(3)] if 0 <= b < 3 else [blank] * 3

    within = [[n for n in range(4) if 1 <= 2 * block + n <= height] for block in range(blocks)]
    beyond = [(0, 0, 0), (3, 1, 2)]
    for block in range(blocks):
        for hb in range(2):
            parts = []
            for x in both:
                by_line = [taps_at(x, n - hb) for n in within[block]]
                parts.append(jnp.concatenate([line[a] for a in range(3) for line in by_line], axis=1))
            inner[block, hb * 3 * chans : (hb + 1) * 3 * chans] = jnp.concatenate([parts[0], parts[1], parts[0]], axis=1)
    for k, (_, _, b) in enumerate(beyond):
        parts = [jnp.concatenate(taps_at(x, b), axis=1) for x in both]
        outer[k] = jnp.concatenate([parts[0], parts[1], parts[0]], axis=1)
    d2, h2, c2 = depth // 2, blocks, down1.shape[2]
    for load in loads[2:5]:
        load.wait()
    for a in range(2):
        for b in range(2):
            for c in range(2):
                spot = pl.ds(((a * 2 + c) * 2 + b) * chans, chans)
                down1_w[spot, 0:c2], down1_w[spot, c2 : 2 * c2] = split(down1[a, (b * 2 + c) * chans : (b * 2 + c + 1) * chans])

    @pl.loop(0, 3)
    def _(a):
        for line in range(1, h2 + 1):
            rows = pl.ds(pl.multiple_of((a * h2 + line - 1) * c2, c2), c2)
            for hb in range(h2):
                for c in range(3):
                    columns = pl.ds((hb * 3 + c) * c2, c2)
                    if 0 <= line - hb < 3:
                        mid_h[rows, columns], mid_l[rows, columns] = split(middle[a * 3 + line - hb, c * c2 : (c + 1) * c2])
                    else:
                        mid_h[rows, columns] = mid_l[rows, columns] = jnp.zeros((c2, c2), BF16)
        rows = pl.ds(pl.multiple_of(a * c2, c2), c2)
        for k, b in ((0, 0), (1, 2)):
            for c in range(3):
                columns = pl.ds(c * c2, c2)
                side_h[k, rows, columns], side_l[k, rows, columns] = split(middle[a * 3 + b, c * c2 : (c + 1) * c2])

    outs = coarse_w.shape[2]
    c3 = coarse.shape[3]

    def prepare_coarse():
        loads[5].wait()

        @pl.loop(0, 3)
        def _(a):
            for b in range(3):
                for c in range(3):
                    high, low = split(coarse_w[a * 3 + b, c * c3 : (c + 1) * c3])
                    spot = (b * 3 + c) * outs
                    coarse_b[a, :, spot : spot + outs] = high
                    coarse_b[a, :, 9 * outs + spot : 10 * outs + spot] = low

    def narrow(ds, hs):
        field_h[ds, hs], field_l[ds, hs] = split(field[ds, hs])

    def across(first, count, d):
        columns = []
        for e in range(2):
            place = (pl.ds(d + e, 3), slice(first, first + count))
            high = field_h[place].reshape(3 * count * chans, width)
            low = field_l[place].reshape(3 * count * chans, width)
            columns.append(jnp.concatenate([high, high, low], axis=0))
        return jnp.concatenate(columns, axis=1)

    dot = functools.partial(jnp.dot, preferred_element_type=F32)
    narrow(slice(1, depth + 1), slice(1, height + 1))
    pairs = [jnp.where(parity == 0, d2 - 1, 0)] + list(range(1, d2 - 1))
    pairs.append(d2 - 1 - pairs[0])
    for n, k in enumerate(pairs):
        if n in (0, d2 - 1):
            for way in range(2):
                mine = (parity == 1 - way) if n == 0 else (parity == way)

                @pl.when(mine)
                def _():
                    arrive(first, True, (way,))
            narrow(pl.ds(jnp.where(k == 0, 0, depth + 1), 1), slice(1, height + 1))
        for block in range(blocks):
            partial[block, k] = dot(inner[block], across(2 * block + within[block][0], len(within[block]), 2 * k))
    hand_on(from_group, crossed, eighth, xsend, xrecv, crossings)
    arrive(first, True, range(2, len(WAYS)))
    for h in (0, height + 1):
        narrow(slice(0, depth + 2), slice(h, h + 1))
    halves = []
    for block in range(blocks):
        n, extra_hb, _ = beyond[block]
        for k in range(d2):
            extra = dot(outer[block], across(2 * block + n, 1, 2 * k))
            row = []
            for e in range(2):
                ends = []
                for hb in range(2):
                    x = partial[block, k, hb * 3 * chans : (hb + 1) * 3 * chans, e * width : (e + 1) * width]
                    if hb == extra_hb:
                        x = x + extra[:, e * width : (e + 1) * width]
                    ends.append(apart(x, width, chans))
                spot = (block * d2 + k) * 2 + e
                turned[spot] = gelu(jnp.concatenate(ends, axis=0)).T
                row += [turned[spot, pl.ds(c, half, stride=2), :] for c in range(2)]
            halves.append(jnp.concatenate(row, axis=1))
    lhs = jnp.concatenate(halves, axis=0)
    wide = dot(stacked(lhs), down1_w[...])
    cells1 = lhs.shape[0]
    total = wide[:cells1, :c2] + wide[:cells1, c2:] + wide[cells1:, :c2]
    total = total.reshape(h2, d2, half, c2)
    for h in range(h2):
        second[1 : d2 + 1, 1 + h] = total[h]
    again = halo(second, 1, second, send2, recv2)
    prepare_coarse()
    def thin(h):
        spot = slice(h * c2, (h + 1) * c2)
        second_h[:, :, spot], second_l[:, :, spot] = split(second[:, h])

    def gathered_taps(low, high):
        parts = []
        for x in (second_h, second_l):
            parts.append(
                jnp.concatenate([x[a : a + d2, :, low:high].reshape(d2 * half, high - low) for a in range(3)], axis=1)
            )
        return jnp.concatenate(parts, axis=0)

    arrive(again, True, range(0, 2))
    for h in range(1, h2 + 1):
        thin(h)
    total = product(gathered_taps(c2, (1 + h2) * c2), (mid_h[...], mid_l[...]))
    hand_on(lambda n, source: crossed[n - 1], forward, half_taps, fsend, frecv, [sibling])
    arrive(again, True, range(2, len(WAYS)))
    for h in (0, h2 + 1):
        thin(h)
    sides = [
        product(gathered_taps(h * c2, (h + 1) * c2), (side_h[k], side_l[k])) for k, h in ((0, 0), (1, h2 + 1))
    ]
    for h in range(h2):
        x = total[:, h * 3 * c2 : (h + 1) * 3 * c2]
        if h == 0:
            x = x + sides[0]
        if h == h2 - 1:
            x = x + sides[1]
        before, _ = beside(x[:, :c2], half)
        _, after = beside(x[:, 2 * c2 :], half)
        level2[h] = gelu(before + x[:, c2 : 2 * c2] + after)
    quarter = half // 2
    lhs = jnp.concatenate(
        [
            level2[h, pl.ds(d * half + c, quarter, stride=2), :]
            for d in range(d2) for h in range(h2) for c in range(2)
        ],
        axis=1,
    )
    lhs = stacked(lhs)
    for made in forward:
        made[0].wait_recv()
    weights = jnp.concatenate(
        [gathered[:, t].reshape(groups * shard.shape[1], c2) for t in range(taps_of)], axis=1
    )
    share = product(lhs, split(weights), (((1,), (1,)), ((), ())))
    coarse[1, pl.ds(g, 1)] = share[None]
    cells = groups * quarter

    sent = []

    def send(there, line, plane, peer, sends, recvs):
        copy = pltpu.make_async_remote_copy(
            src_ref=coarse.at[1, line], dst_ref=coarse.at[plane, line], send_sem=sends, recv_sem=recvs,
            device_id=peer, device_id_type=MESH,
        )

        @pl.when(there)
        def _():
            copy.start()

        sent.append((there, copy))

    def sideways(n):
        for k, ds in enumerate((1, -1)):
            send(exists(ds, 0), order[n], 1 - ds, (s + ds, g), nsend.at[k, n], nrecv.at[1 - ds, order[n]])

    for k, dg in enumerate(d for d in range(1 - groups, groups) if d):
        send(exists(0, dg), g, 1, (s, g + dg), csend.at[k], crecv.at[g])
    sideways(0)

    def landed(n, plane):
        line = order[n]
        mine = isinstance(plane, int) and plane == 1
        sems = crecv.at[line] if mine else nrecv.at[plane, line]
        copy = pltpu.make_async_remote_copy(
            src_ref=coarse.at[plane, line], dst_ref=coarse.at[plane, line], send_sem=csend.at[0], recv_sem=sems,
            device_id=(s, g), device_id_type=MESH,
        )
        if mine:
            copy.wait_recv()
        else:
            @pl.when(exists(plane - 1, 0))
            def _():
                copy.wait_recv()

    def terms(ns, plane):
        x = jnp.concatenate([coarse[plane, pl.ds(order[n], 1)][0] for n in ns], axis=0)
        size = len(ns) * quarter
        wide = dot(stacked(x), coarse_b[plane])
        span = 9 * outs
        wide = wide[:size, :span] + wide[:size, span:] + wide[size:, :span]
        for k, n in enumerate(ns):
            for b in range(3):
                spot = pl.ds(pl.multiple_of((order[n] + 2 - b) * quarter, quarter), quarter)
                sums[spot] = sums[spot] + wide[k * quarter : (k + 1) * quarter, b * 3 * outs : (b + 1) * 3 * outs]

    def own(ns):
        for n in ns:
            if n:
                landed(n, 1)
                sideways(n)
        terms(ns, 1)

    def others(ns):
        for plane in (2 - 2 * parity, 2 * parity):
            for n in ns:
                landed(n, plane)
            terms(ns, plane)

    for plane in (0, 2):
        @pl.when(jnp.logical_not(exists(plane - 1, 0)))
        def _():
            coarse[plane] = jnp.zeros(coarse.shape[1:], F32)

    sums[...] = jnp.zeros(sums.shape, F32)
    stages = [[0]] + [list(range(n, min(n + 2, groups))) for n in range(1, groups, 2)]
    for k, stage in enumerate(stages):
        own(stage)
        if 0 < k < len(stages) - 1:
            others(stages[k - 1])
    for stage in stages[-2:]:
        others(stage)
    x = sums[quarter : quarter + cells]
    before, _ = beside(x[:, :outs], quarter)
    _, after = beside(x[:, 2 * outs :], quarter)
    out[...] = gelu(before + x[:, outs : 2 * outs] + after).T

    arrive(first, False)
    arrive(again, False)
    for copy in sum(crossed + forward, []):
        copy.wait_send()
    for there, copy in spread + sent:
        @pl.when(there)
        def _():
            copy.wait_send()


def per_device(slabs, groups, volume, conv_fine, down_first, conv_middle, down_second, conv_coarse):
    c1, depth, height, width = volume.shape
    c2, c3, c4 = down_first.shape[4], conv_coarse.shape[3], conv_coarse.shape[4]
    half, quarter = width // 2, width // 4
    d2, h2 = depth // 2, height // 2
    part = down_second.shape[4]
    cells = groups * quarter
    vol = volume.reshape(c1 * depth * height, width)
    fine = conv_fine.reshape(27, c1, c1)
    down1 = down_first.reshape(2, 4 * c1, c2)
    middle = conv_middle.reshape(9, 3 * c2, c2)
    shard = jnp.swapaxes(down_second, 3, 4).reshape(8, part, c2)
    coarse_w = conv_coarse.reshape(9, 3 * c3, c4)
    V = pltpu.VMEM
    vmem, away = pl.BlockSpec(memory_space=pltpu.VMEM), pl.BlockSpec(memory_space=pl.ANY)
    dma = pltpu.SemaphoreType.DMA
    result = pl.pallas_call(
        functools.partial(kernel, slabs, groups),
        out_shape=pltpu.VMEM((c4, cells), F32),
        in_specs=[away] * 6,
        out_specs=vmem,
        scratch_shapes=[
            V(vol.shape, F32),
            V(fine.shape, F32),
            V((depth + 2, height + 2, c1, width), F32),
            V((depth + 2, height + 2, c1, width), BF16),
            V((depth + 2, height + 2, c1, width), BF16),
            V((2, 6 * c1, 27 * c1), BF16),
            V((2, 3 * c1, 9 * c1), BF16),
            V((2, d2, 6 * c1, 2 * width), F32),
            V((2 * d2 * 2, width, 2 * c1), F32),
            V(down1.shape, F32),
            V((8 * c1, 2 * c2), BF16),
            V(middle.shape, F32),
            V((3 * h2 * c2, 3 * h2 * c2), BF16),
            V((3 * h2 * c2, 3 * h2 * c2), BF16),
            V((2, 3 * c2, 3 * c2), BF16),
            V((2, 3 * c2, 3 * c2), BF16),
            V((d2 + 2, h2 + 2, half, c2), F32),
            V((d2 + 2, half, (h2 + 2) * c2), BF16),
            V((d2 + 2, half, (h2 + 2) * c2), BF16),
            V((h2, d2 * half, c2), F32),
            V((groups,) + shard.shape, F32),
            V(coarse_w.shape, F32),
            V((3, c3, 18 * c4), BF16),
            V((3, groups, quarter, c3), F32),
            V((cells + 2 * quarter, 3 * c4), F32),
            dma((6,)),
            pltpu.SemaphoreType.REGULAR((max(1, groups - 2),)),
            dma((8,)), dma((8,)), dma((8,)), dma((8,)),
            dma((2 * groups,)), dma((groups,)), dma((groups, 3)), dma((groups, 3)), dma((groups, 1)), dma((groups, 1)), dma((2 * groups,)), dma((groups,)),
            dma((2, groups)), dma((3, groups)),
        ],
        compiler_params=pltpu.CompilerParams(
            collective_id=0, has_side_effects=True, vmem_limit_bytes=60 * 1024 * 1024
        ),
    )(vol, fine, down1, middle, shard, coarse_w)
    return result.reshape(c4, 1, cells)


def solution(mesh):
    placed = (
        P(None, "slab", "grp", None),
        P(),
        P(),
        P(),
        P(None, None, None, None, "grp"),
        P(None, None, None, None, "grp"),
    )
    body = functools.partial(per_device, mesh.shape["slab"], mesh.shape["grp"])
    return jax.shard_map(
        body, mesh=mesh, in_specs=placed, out_specs=P("grp", "slab", None), check_vma=False
    )
```

```python
import functools

import jax
import jax.numpy as jnp
from jax import lax
from jax.experimental import pallas as pl
from jax.experimental.pallas import tpu as pltpu
from jax.sharding import PartitionSpec as P

MESH = pl.DeviceIdType.MESH
F32, BF16 = jnp.float32, jnp.bfloat16
WAYS = ((1, 0), (-1, 0), (0, 1), (0, -1), (1, 1), (1, -1), (-1, 1), (-1, -1))


def split(x):
    high = x.astype(BF16)
    return high, (x - high.astype(F32)).astype(BF16)


def stacked(x):
    return jnp.concatenate(split(x), axis=0)


def product(both, weights, dims=(((1,), (0,)), ((), ()))):
    dot = functools.partial(lax.dot_general, dimension_numbers=dims, preferred_element_type=F32)
    rows = both.shape[0] // 2
    wide = dot(both, weights[0])
    return wide[:rows] + wide[rows:] + dot(both[:rows], weights[1])


def plus(total, term):
    return term if total is None else total + term


def gelu(x):
    return 0.5 * x * (1.0 + lax.erf(x * (0.5**0.5)))


def apart(x, width, chans):
    lane = lax.broadcasted_iota(jnp.int32, (chans, width), 1)
    before = jnp.where(lane == 0, 0.0, pltpu.roll(x[:chans], 1, 1))
    after = jnp.where(lane == width - 1, 0.0, pltpu.roll(x[2 * chans :], width - 1, 1))
    return before + x[chans : 2 * chans] + after


def beside(x, span):
    at = lax.rem(lax.broadcasted_iota(jnp.int32, x.shape, 0), span)
    before = jnp.where(at == 0, 0.0, pltpu.roll(x, 1, 0))
    after = jnp.where(at == span - 1, 0.0, pltpu.roll(x, x.shape[0] - 1, 0))
    return before, after


def kernel(
    slabs, groups,
    vol_hbm, fine_hbm, down1_hbm, middle_hbm, shard, coarse_hbm,
    out,
    vol, fine, field, field_h, field_l, inner, outer, partial, turned, down1, down1_w, middle,
    mid_h, mid_l, side_h, side_l, second, second_h, second_l, level2, gathered, coarse_w, coarse_b,
    coarse, sums,
    load_sem, ready, face_sem, recv1, recv2, spread_sem, wrecv, xrecv, frecv, crecv, nrecv,
):
    s, g = lax.axis_index("slab"), lax.axis_index("grp")
    depth, height, chans, width = (field.shape[0] - 2, field.shape[1] - 2) + field.shape[2:]
    half = width // 2

    loads = [
        pltpu.make_async_copy(vol_hbm, vol, load_sem.at[3]),
        pltpu.make_async_copy(fine_hbm, fine, load_sem.at[4]),
        pltpu.make_async_copy(shard, gathered.at[g], load_sem.at[5]),
        pltpu.make_async_copy(down1_hbm, down1, load_sem.at[0]),
        pltpu.make_async_copy(middle_hbm, middle, load_sem.at[1]),
        pltpu.make_async_copy(coarse_hbm, coarse_w, load_sem.at[2]),
    ]
    for load in loads:
        load.start()

    def exists(ds, dg):
        return (s + ds >= 0) & (s + ds < slabs) & (g + dg >= 0) & (g + dg < groups)

    barrier = pltpu.get_barrier_semaphore()
    heard = jnp.int32(0)
    for ds, dg in WAYS[:4]:
        there = exists(ds, dg)
        heard = heard + there.astype(jnp.int32)

        @pl.when(there)
        def _():
            pl.semaphore_signal(barrier, inc=1, device_id=(s + ds, g + dg), device_id_type=MESH)

    sibling = s + 1 - 2 * lax.rem(s, 2)
    low, high = lax.rem(s // 2, 2), lax.rem(s // 4, 2)
    crossings = [s + 2 - 4 * low, s + 4 - 8 * high, s + 6 - 4 * low - 8 * high]
    for peer in crossings:
        pl.semaphore_signal(barrier, inc=1, device_id=(peer, g), device_id_type=MESH)
    pl.semaphore_wait(barrier, heard + len(crossings))

    taps_of = shard.shape[0]
    parity = lax.rem(s, 2)
    eighth = pl.ds((parity * 4 + lax.rem(s // 2, 4)) * (taps_of // 8), taps_of // 8)
    half_taps = pl.ds(parity * (taps_of // 2), taps_of // 2)
    def nth(n):
        spare = jnp.minimum(g, groups - 1 - g)
        near = (n + 1) // 2 if n % 2 else -(n // 2)
        away = jnp.where(2 * g < groups - 1, 1, -1)
        return g + jnp.where(n <= 2 * spare, near, away * (n - spare))

    order = [nth(n) for n in range(groups)]
    rounds = max(1, groups - 2)

    def settle(sem, view):
        pltpu.make_async_remote_copy(
            src_ref=view, dst_ref=view, send_sem=sem, recv_sem=sem, device_id=(s, g), device_id_type=MESH
        ).wait_recv()

    def spread_to(n):
        pltpu.make_async_remote_copy(
            src_ref=shard.at[eighth], dst_ref=gathered.at[g, eighth],
            send_sem=spread_sem.at[0], recv_sem=wrecv.at[lax.rem(g - order[n] - 1 + groups, groups)],
            device_id=(s, order[n]), device_id_type=MESH,
        ).start()

    def announce(n):
        for ds, dg in WAYS[:4] if n == 0 else WAYS[2:4]:
            @pl.when(exists(ds, dg))
            def _():
                pl.semaphore_signal(ready.at[n], inc=1, device_id=(s + ds, g + dg), device_id_type=MESH)

    def listen(n):
        count = jnp.int32(0)
        for ds, dg in WAYS[:4] if n == 0 else WAYS[2:4]:
            count = count + exists(ds, dg).astype(jnp.int32)
        pl.semaphore_wait(ready.at[n], count)

    announce(0)
    spread_to(1)

    loads[0].wait()
    lines = depth * height
    for r in range(lines):
        field[1 + r // height, 1 + r % height] = vol[pl.ds(r, chans, stride=lines), :]
    def part(way, size, offset):
        if way == 0:
            return pl.ds(offset, size)
        return pl.ds(offset + (size - 1 if way > 0 else 0), 1)

    def landing(way, size):
        if way == 0:
            return pl.ds(1, size)
        return pl.ds(0 if way > 0 else size + 1, 1)

    def halo(src, offset, buf, sends, recvs, between=None):
        nd, nh = buf.shape[0] - 2, buf.shape[1] - 2
        copies = []
        for k, (ds, dg) in enumerate(WAYS):
            if k == 4 and between is not None:
                between()
            copies.append(
                pltpu.make_async_remote_copy(
                    src_ref=src.at[part(ds, nd, offset), part(dg, nh, offset)],
                    dst_ref=buf.at[landing(ds, nd), landing(dg, nh)],
                    send_sem=sends.at[k],
                    recv_sem=recvs.at[k],
                    device_id=(s + ds, g + dg),
                    device_id_type=MESH,
                )
            )

            @pl.when(exists(ds, dg))
            def _():
                copies[k].start()

            @pl.when(jnp.logical_not(exists(-ds, -dg)))
            def _():
                piece = (landing(ds, nd), landing(dg, nh))
                shape = (piece[0].size, piece[1].size) + buf.shape[2:]
                buf[piece[0], piece[1]] = jnp.zeros(shape, F32)

        return copies

    def arrive(copies, received, ways=range(len(WAYS))):
        for k in ways:
            ds, dg = WAYS[k]
            if received:
                @pl.when(exists(-ds, -dg))
                def _():
                    copies[k].wait_recv()
            else:
                @pl.when(exists(ds, dg))
                def _():
                    copies[k].wait_send()

    def further():
        for n in range(rounds):
            listen(n)
            if n + 1 < rounds:
                announce(n + 1)
            if n + 2 < groups:
                spread_to(n + 2)

    first = halo(field, 1, field, face_sem, recv1, further)

    foreign = slice(0, groups - 1)

    def hand_on(piece, sends, recvs, peers, spread=False):
        for n in range(1, groups):
            source = order[n]
            if spread:
                settle(wrecv.at[lax.rem(source - g - 1 + groups, groups)], gathered.at[source, eighth])
            for peer in peers:
                pltpu.make_async_remote_copy(
                    src_ref=gathered.at[source, piece], dst_ref=gathered.at[source, piece],
                    send_sem=sends, recv_sem=recvs, device_id=(peer, g), device_id_type=MESH,
                ).start()

    loads[1].wait()
    blocks = height // 2
    blank = jnp.zeros((3 * chans, chans), BF16)
    wide = jnp.concatenate(
        [
            jnp.concatenate([fine[ab * 3 + c] for c in range(3)], axis=1)
            for ab in range(9)
        ],
        axis=0,
    )
    both = split(wide.T)

    def taps_at(x, b):
        return [x[:, (a * 3 + b) * chans : (a * 3 + b + 1) * chans] for a in range(3)] if 0 <= b < 3 else [blank] * 3

    within = [[n for n in range(4) if 1 <= 2 * block + n <= height] for block in range(blocks)]
    beyond = [(0, 0, 0), (3, 1, 2)]
    for block in range(blocks):
        for hb in range(2):
            parts = []
            for x in both:
                by_line = [taps_at(x, n - hb) for n in within[block]]
                parts.append(jnp.concatenate([line[a] for a in range(3) for line in by_line], axis=1))
            inner[block, hb * 3 * chans : (hb + 1) * 3 * chans] = jnp.concatenate([parts[0], parts[1], parts[0]], axis=1)
    for k, (_, _, b) in enumerate(beyond):
        parts = [jnp.concatenate(taps_at(x, b), axis=1) for x in both]
        outer[k] = jnp.concatenate([parts[0], parts[1], parts[0]], axis=1)
    d2, h2, c2 = depth // 2, blocks, down1.shape[2]
    for load in loads[2:5]:
        load.wait()
    for a in range(2):
        for b in range(2):
            for c in range(2):
                spot = pl.ds(((a * 2 + c) * 2 + b) * chans, chans)
                down1_w[spot, 0:c2], down1_w[spot, c2 : 2 * c2] = split(down1[a, (b * 2 + c) * chans : (b * 2 + c + 1) * chans])

    @pl.loop(0, 3)
    def _(a):
        for line in range(1, h2 + 1):
            rows = pl.ds(pl.multiple_of((a * h2 + line - 1) * c2, c2), c2)
            for hb in range(h2):
                for c in range(3):
                    columns = pl.ds((hb * 3 + c) * c2, c2)
                    if 0 <= line - hb < 3:
                        mid_h[rows, columns], mid_l[rows, columns] = split(middle[a * 3 + line - hb, c * c2 : (c + 1) * c2])
                    else:
                        mid_h[rows, columns] = mid_l[rows, columns] = jnp.zeros((c2, c2), BF16)
        rows = pl.ds(pl.multiple_of(a * c2, c2), c2)
        for k, b in ((0, 0), (1, 2)):
            for c in range(3):
                columns = pl.ds(c * c2, c2)
                side_h[k, rows, columns], side_l[k, rows, columns] = split(middle[a * 3 + b, c * c2 : (c + 1) * c2])

    outs = coarse_w.shape[2]
    c3 = coarse.shape[3]

    def prepare_coarse():
        loads[5].wait()

        @pl.loop(0, 3)
        def _(a):
            for b in range(3):
                for c in range(3):
                    high, low = split(coarse_w[a * 3 + b, c * c3 : (c + 1) * c3])
                    spot = (b * 3 + c) * outs
                    coarse_b[a, :, spot : spot + outs] = high
                    coarse_b[a, :, 9 * outs + spot : 10 * outs + spot] = low

    def narrow(ds, hs):
        field_h[ds, hs], field_l[ds, hs] = split(field[ds, hs])

    def across(first, count, d):
        columns = []
        for e in range(2):
            place = (pl.ds(d + e, 3), slice(first, first + count))
            high = field_h[place].reshape(3 * count * chans, width)
            low = field_l[place].reshape(3 * count * chans, width)
            columns.append(jnp.concatenate([high, high, low], axis=0))
        return jnp.concatenate(columns, axis=1)

    dot = functools.partial(jnp.dot, preferred_element_type=F32)
    narrow(slice(1, depth + 1), slice(1, height + 1))
    pairs = [jnp.where(parity == 0, d2 - 1, 0)] + list(range(1, d2 - 1))
    pairs.append(d2 - 1 - pairs[0])
    for n, k in enumerate(pairs):
        if n in (0, d2 - 1):
            for way in range(2):
                mine = (parity == 1 - way) if n == 0 else (parity == way)

                @pl.when(mine)
                def _():
                    arrive(first, True, (way,))
            narrow(pl.ds(jnp.where(k == 0, 0, depth + 1), 1), slice(1, height + 1))
        for block in range(blocks):
            partial[block, k] = dot(inner[block], across(2 * block + within[block][0], len(within[block]), 2 * k))
    hand_on(eighth, load_sem.at[0], xrecv.at[0], crossings, True)
    arrive(first, True, range(2, len(WAYS)))
    for h in (0, height + 1):
        narrow(slice(0, depth + 2), slice(h, h + 1))
    halves = []
    for block in range(blocks):
        n, extra_hb, _ = beyond[block]
        for k in range(d2):
            extra = dot(outer[block], across(2 * block + n, 1, 2 * k))
            row = []
            for e in range(2):
                ends = []
                for hb in range(2):
                    x = partial[block, k, hb * 3 * chans : (hb + 1) * 3 * chans, e * width : (e + 1) * width]
                    if hb == extra_hb:
                        x = x + extra[:, e * width : (e + 1) * width]
                    ends.append(apart(x, width, chans))
                spot = (block * d2 + k) * 2 + e
                turned[spot] = gelu(jnp.concatenate(ends, axis=0)).T
                row += [turned[spot, pl.ds(c, half, stride=2), :] for c in range(2)]
            halves.append(jnp.concatenate(row, axis=1))
    lhs = jnp.concatenate(halves, axis=0)
    wide = dot(stacked(lhs), down1_w[...])
    cells1 = lhs.shape[0]
    total = wide[:cells1, :c2] + wide[:cells1, c2:] + wide[cells1:, :c2]
    total = total.reshape(h2, d2, half, c2)
    for h in range(h2):
        second[1 : d2 + 1, 1 + h] = total[h]
    arrive(first, False)
    again = halo(second, 1, second, face_sem, recv2)
    prepare_coarse()
    def thin(h):
        spot = slice(h * c2, (h + 1) * c2)
        second_h[:, :, spot], second_l[:, :, spot] = split(second[:, h])

    def gathered_taps(low, high):
        parts = []
        for x in (second_h, second_l):
            parts.append(
                jnp.concatenate([x[a : a + d2, :, low:high].reshape(d2 * half, high - low) for a in range(3)], axis=1)
            )
        return jnp.concatenate(parts, axis=0)

    arrive(again, True, range(0, 2))
    for h in range(1, h2 + 1):
        thin(h)
    total = product(gathered_taps(c2, (1 + h2) * c2), (mid_h[...], mid_l[...]))
    settle(xrecv.at[0], gathered.at[foreign, 0 : 3 * (taps_of // 8)])
    hand_on(half_taps, load_sem.at[1], frecv.at[0], [sibling])
    arrive(again, True, range(2, len(WAYS)))
    for h in (0, h2 + 1):
        thin(h)
    sides = [
        product(gathered_taps(h * c2, (h + 1) * c2), (side_h[k], side_l[k])) for k, h in ((0, 0), (1, h2 + 1))
    ]
    for h in range(h2):
        x = total[:, h * 3 * c2 : (h + 1) * 3 * c2]
        if h == 0:
            x = x + sides[0]
        if h == h2 - 1:
            x = x + sides[1]
        before, _ = beside(x[:, :c2], half)
        _, after = beside(x[:, 2 * c2 :], half)
        level2[h] = gelu(before + x[:, c2 : 2 * c2] + after)
    quarter = half // 2
    lhs = jnp.concatenate(
        [
            level2[h, pl.ds(d * half + c, quarter, stride=2), :]
            for d in range(d2) for h in range(h2) for c in range(2)
        ],
        axis=1,
    )
    lhs = stacked(lhs)
    settle(frecv.at[0], gathered.at[foreign, 0 : taps_of // 2])
    filters = jnp.concatenate(
        [gathered[:, t].reshape(groups * shard.shape[1], c2) for t in range(taps_of)], axis=1
    )
    share = product(lhs, split(filters), (((1,), (1,)), ((), ())))
    coarse[1, pl.ds(g, 1)] = share[None]
    cells = groups * quarter

    def sideways(n):
        for k, ds in enumerate((1, -1)):
            copy = pltpu.make_async_remote_copy(
                src_ref=coarse.at[1, order[n]], dst_ref=coarse.at[1 - ds, order[n]],
                send_sem=load_sem.at[3 + k], recv_sem=nrecv.at[k, (n + 1) // 2],
                device_id=(s + ds, g), device_id_type=MESH,
            )

            @pl.when(exists(ds, 0))
            def _():
                copy.start()

    for n in range(groups - 1, 0, -1):
        pltpu.make_async_remote_copy(
            src_ref=coarse.at[1, g], dst_ref=coarse.at[1, g],
            send_sem=load_sem.at[2], recv_sem=crecv.at[lax.rem(g - order[n] - 1 + groups, groups)],
            device_id=(s, order[n]), device_id_type=MESH,
        ).start()
    sideways(0)

    def terms(ns, plane):
        x = jnp.concatenate([coarse[plane, pl.ds(order[n], 1)][0] for n in ns], axis=0)
        size = len(ns) * quarter
        wide = dot(stacked(x), coarse_b[plane])
        span = 9 * outs
        wide = wide[:size, :span] + wide[:size, span:] + wide[size:, :span]
        for k, n in enumerate(ns):
            for b in range(3):
                spot = pl.ds(pl.multiple_of((order[n] + 2 - b) * quarter, quarter), quarter)
                sums[spot] = sums[spot] + wide[k * quarter : (k + 1) * quarter, b * 3 * outs : (b + 1) * 3 * outs]

    def own(ns):
        for n in ns:
            if n:
                settle(crecv.at[lax.rem(order[n] - g - 1 + groups, groups)], coarse.at[1, order[n]])
                sideways(n)
        terms(ns, 1)

    def others(ns):
        for plane in (2 - 2 * parity, 2 * parity):

            @pl.when(exists(plane - 1, 0))
            def _():
                settle(nrecv.at[plane // 2, (ns[0] + 1) // 2], coarse.at[1, 0 : len(ns)])

            terms(ns, plane)

    for plane in (0, 2):
        @pl.when(jnp.logical_not(exists(plane - 1, 0)))
        def _():
            coarse[plane] = jnp.zeros(coarse.shape[1:], F32)

    sums[...] = jnp.zeros(sums.shape, F32)
    stages = [[0]] + [list(range(n, min(n + 2, groups))) for n in range(1, groups, 2)]
    for k, stage in enumerate(stages):
        own(stage)
        if 0 < k < len(stages) - 1:
            others(stages[k - 1])
    for stage in stages[-2:]:
        others(stage)
    x = sums[quarter : quarter + cells]
    before, _ = beside(x[:, :outs], quarter)
    _, after = beside(x[:, 2 * outs :], quarter)
    out[...] = gelu(before + x[:, outs : 2 * outs] + after).T

    arrive(again, False)
    settle(spread_sem.at[0], gathered.at[foreign, 0 : taps_of // 8])
    settle(load_sem.at[0], gathered.at[foreign, 0 : 3 * (taps_of // 8)])
    settle(load_sem.at[1], gathered.at[foreign, 0 : taps_of // 2])
    settle(load_sem.at[2], coarse.at[1, 0 : groups - 1])
    for k, ds in enumerate((1, -1)):
        @pl.when(exists(ds, 0))
        def _():
            settle(load_sem.at[3 + k], coarse.at[1])


def per_device(slabs, groups, volume, conv_fine, down_first, conv_middle, down_second, conv_coarse):
    c1, depth, height, width = volume.shape
    c2, c3, c4 = down_first.shape[4], conv_coarse.shape[3], conv_coarse.shape[4]
    half, quarter = width // 2, width // 4
    d2, h2 = depth // 2, height // 2
    part = down_second.shape[4]
    cells = groups * quarter
    vol = volume.reshape(c1 * depth * height, width)
    fine = conv_fine.reshape(27, c1, c1)
    down1 = down_first.reshape(2, 4 * c1, c2)
    middle = conv_middle.reshape(9, 3 * c2, c2)
    shard = jnp.swapaxes(down_second, 3, 4).reshape(8, part, c2)
    coarse_w = conv_coarse.reshape(9, 3 * c3, c4)
    V = pltpu.VMEM
    vmem, away = pl.BlockSpec(memory_space=pltpu.VMEM), pl.BlockSpec(memory_space=pl.ANY)
    dma = pltpu.SemaphoreType.DMA
    result = pl.pallas_call(
        functools.partial(kernel, slabs, groups),
        out_shape=pltpu.VMEM((c4, cells), F32),
        in_specs=[away] * 6,
        out_specs=vmem,
        scratch_shapes=[
            V(vol.shape, F32),
            V(fine.shape, F32),
            V((depth + 2, height + 2, c1, width), F32),
            V((depth + 2, height + 2, c1, width), BF16),
            V((depth + 2, height + 2, c1, width), BF16),
            V((2, 6 * c1, 27 * c1), BF16),
            V((2, 3 * c1, 9 * c1), BF16),
            V((2, d2, 6 * c1, 2 * width), F32),
            V((2 * d2 * 2, width, 2 * c1), F32),
            V(down1.shape, F32),
            V((8 * c1, 2 * c2), BF16),
            V(middle.shape, F32),
            V((3 * h2 * c2, 3 * h2 * c2), BF16),
            V((3 * h2 * c2, 3 * h2 * c2), BF16),
            V((2, 3 * c2, 3 * c2), BF16),
            V((2, 3 * c2, 3 * c2), BF16),
            V((d2 + 2, h2 + 2, half, c2), F32),
            V((d2 + 2, half, (h2 + 2) * c2), BF16),
            V((d2 + 2, half, (h2 + 2) * c2), BF16),
            V((h2, d2 * half, c2), F32),
            V((groups,) + shard.shape, F32),
            V(coarse_w.shape, F32),
            V((3, c3, 18 * c4), BF16),
            V((3, groups, quarter, c3), F32),
            V((cells + 2 * quarter, 3 * c4), F32),
            dma((6,)),
            pltpu.SemaphoreType.REGULAR((max(1, groups - 2),)),
            dma((8,)), dma((8,)), dma((8,)),
            dma((1,)), dma((groups - 1,)), dma((1,)), dma((1,)), dma((groups - 1,)), dma((2, 1 + groups // 2)),
        ],
        compiler_params=pltpu.CompilerParams(
            collective_id=0, has_side_effects=True, vmem_limit_bytes=60 * 1024 * 1024
        ),
    )(vol, fine, down1, middle, shard, coarse_w)
    return result.reshape(c4, 1, cells)


def solution(mesh):
    placed = (
        P(None, "slab", "grp", None),
        P(),
        P(),
        P(),
        P(None, None, None, None, "grp"),
        P(None, None, None, None, "grp"),
    )
    body = functools.partial(per_device, mesh.shape["slab"], mesh.shape["grp"])
    return jax.shard_map(
        body, mesh=mesh, in_specs=placed, out_specs=P("grp", "slab", None), check_vma=False
    )
```

```python
import functools

import jax
import jax.numpy as jnp
from jax import lax
from jax.experimental import pallas as pl
from jax.experimental.pallas import tpu as pltpu
from jax.sharding import PartitionSpec as P

MESH = pl.DeviceIdType.MESH
F32, BF16 = jnp.float32, jnp.bfloat16
WAYS = ((1, 0), (-1, 0), (0, 1), (0, -1), (1, 1), (1, -1), (-1, 1), (-1, -1))


def split(x):
    high = x.astype(BF16)
    return high, (x - high.astype(F32)).astype(BF16)


def stacked(x):
    return jnp.concatenate(split(x), axis=0)


def product(both, weights, dims=(((1,), (0,)), ((), ()))):
    dot = functools.partial(lax.dot_general, dimension_numbers=dims, preferred_element_type=F32)
    rows = both.shape[0] // 2
    wide = dot(both, weights[0])
    return wide[:rows] + wide[rows:] + dot(both[:rows], weights[1])


def plus(total, term):
    return term if total is None else total + term


def gelu(x):
    return 0.5 * x * (1.0 + lax.erf(x * (0.5**0.5)))


def apart(x, width, chans):
    lane = lax.broadcasted_iota(jnp.int32, (chans, width), 1)
    before = jnp.where(lane == 0, 0.0, pltpu.roll(x[:chans], 1, 1))
    after = jnp.where(lane == width - 1, 0.0, pltpu.roll(x[2 * chans :], width - 1, 1))
    return before + x[chans : 2 * chans] + after


def beside(x, span):
    at = lax.rem(lax.broadcasted_iota(jnp.int32, x.shape, 0), span)
    before = jnp.where(at == 0, 0.0, pltpu.roll(x, 1, 0))
    after = jnp.where(at == span - 1, 0.0, pltpu.roll(x, x.shape[0] - 1, 0))
    return before, after


def kernel(
    slabs, groups,
    vol_hbm, fine_hbm, down1_hbm, middle_hbm, shard, coarse_hbm,
    out,
    vol, fine, field, field_h, field_l, inner, outer, partial, turned, down1, down1_w, middle,
    mid_h, mid_l, side_h, side_l, second, second_h, second_l, level2, gathered, coarse_w, coarse_b,
    coarse, sums,
    load_sem, ready, face_sem, recv1, recv2, spread_sem, wrecv, xrecv, frecv, crecv, nrecv,
):
    s, g = lax.axis_index("slab"), lax.axis_index("grp")
    depth, height, chans, width = (field.shape[0] - 2, field.shape[1] - 2) + field.shape[2:]
    half = width // 2

    loads = [
        pltpu.make_async_copy(vol_hbm, vol, load_sem.at[3]),
        pltpu.make_async_copy(fine_hbm, fine, load_sem.at[4]),
        pltpu.make_async_copy(shard, gathered.at[g], load_sem.at[5]),
        pltpu.make_async_copy(down1_hbm, down1, load_sem.at[0]),
        pltpu.make_async_copy(middle_hbm, middle, load_sem.at[1]),
        pltpu.make_async_copy(coarse_hbm, coarse_w, load_sem.at[2]),
    ]
    for load in loads:
        load.start()

    def exists(ds, dg):
        return (s + ds >= 0) & (s + ds < slabs) & (g + dg >= 0) & (g + dg < groups)

    barrier = pltpu.get_barrier_semaphore()
    heard = jnp.int32(0)
    for ds, dg in WAYS[:4]:
        there = exists(ds, dg)
        heard = heard + there.astype(jnp.int32)

        @pl.when(there)
        def _():
            pl.semaphore_signal(barrier, inc=1, device_id=(s + ds, g + dg), device_id_type=MESH)

    sibling = s + 1 - 2 * lax.rem(s, 2)
    low, high = lax.rem(s // 2, 2), lax.rem(s // 4, 2)
    crossings = [s + 2 - 4 * low, s + 4 - 8 * high, s + 6 - 4 * low - 8 * high]
    for peer in crossings:
        pl.semaphore_signal(barrier, inc=1, device_id=(peer, g), device_id_type=MESH)
    pl.semaphore_wait(barrier, heard + len(crossings))

    taps_of = shard.shape[0]
    parity = lax.rem(s, 2)
    eighth = pl.ds((parity * 4 + lax.rem(s // 2, 4)) * (taps_of // 8), taps_of // 8)
    half_taps = pl.ds(parity * (taps_of // 2), taps_of // 2)
    def nth(n):
        spare = jnp.minimum(g, groups - 1 - g)
        near = (n + 1) // 2 if n % 2 else -(n // 2)
        away = jnp.where(2 * g < groups - 1, 1, -1)
        return g + jnp.where(n <= 2 * spare, near, away * (n - spare))

    order = [nth(n) for n in range(groups)]
    rounds = max(1, groups - 2)

    def settle(sem, view):
        pltpu.make_async_remote_copy(
            src_ref=view, dst_ref=view, send_sem=sem, recv_sem=sem, device_id=(s, g), device_id_type=MESH
        ).wait_recv()

    def spread_to(n, there=True):
        copy = pltpu.make_async_remote_copy(
            src_ref=shard.at[eighth], dst_ref=gathered.at[g, eighth],
            send_sem=spread_sem.at[0], recv_sem=wrecv.at[lax.rem(g - order[n] - 1 + groups, groups)],
            device_id=(s, order[n]), device_id_type=MESH,
        )

        @pl.when(there)
        def _():
            copy.start()

    def announce(n):
        for ds, dg in WAYS[:4] if n == 0 else WAYS[2:4]:
            @pl.when(exists(ds, dg))
            def _():
                pl.semaphore_signal(ready.at[n], inc=1, device_id=(s + ds, g + dg), device_id_type=MESH)

    def listen(n):
        count = jnp.int32(0)
        for ds, dg in WAYS[:4] if n == 0 else WAYS[2:4]:
            count = count + exists(ds, dg).astype(jnp.int32)
        pl.semaphore_wait(ready.at[n], count)

    announce(0)
    spread_to(1)
    inside = (g > 0) & (g < groups - 1)
    if groups > 2:
        spread_to(2, inside)

    loads[0].wait()
    lines = depth * height
    for r in range(lines):
        field[1 + r // height, 1 + r % height] = vol[pl.ds(r, chans, stride=lines), :]
    def part(way, size, offset):
        if way == 0:
            return pl.ds(offset, size)
        return pl.ds(offset + (size - 1 if way > 0 else 0), 1)

    def landing(way, size):
        if way == 0:
            return pl.ds(1, size)
        return pl.ds(0 if way > 0 else size + 1, 1)

    def halo(src, offset, buf, sends, recvs, between=None):
        nd, nh = buf.shape[0] - 2, buf.shape[1] - 2
        copies = []
        for k, (ds, dg) in enumerate(WAYS):
            if k == 4 and between is not None:
                between()
            copies.append(
                pltpu.make_async_remote_copy(
                    src_ref=src.at[part(ds, nd, offset), part(dg, nh, offset)],
                    dst_ref=buf.at[landing(ds, nd), landing(dg, nh)],
                    send_sem=sends.at[k],
                    recv_sem=recvs.at[k],
                    device_id=(s + ds, g + dg),
                    device_id_type=MESH,
                )
            )

            @pl.when(exists(ds, dg))
            def _():
                copies[k].start()

            @pl.when(jnp.logical_not(exists(-ds, -dg)))
            def _():
                piece = (landing(ds, nd), landing(dg, nh))
                shape = (piece[0].size, piece[1].size) + buf.shape[2:]
                buf[piece[0], piece[1]] = jnp.zeros(shape, F32)

        return copies

    def arrive(copies, received, ways=range(len(WAYS))):
        for k in ways:
            ds, dg = WAYS[k]
            if received:
                @pl.when(exists(-ds, -dg))
                def _():
                    copies[k].wait_recv()
            else:
                @pl.when(exists(ds, dg))
                def _():
                    copies[k].wait_send()

    def vouch(n):
        listen(n)
        if n + 1 < rounds:
            announce(n + 1)
        if n + 2 < groups:
            spread_to(n + 2, jnp.logical_not(inside) if n == 0 else True)

    first = halo(field, 1, field, face_sem, recv1, lambda: vouch(0))

    foreign = slice(0, groups - 1)

    def hand_on(piece, sends, recvs, peers, spread=False, ns=range(1, groups)):
        for n in ns:
            source = order[n]
            if spread:
                settle(wrecv.at[lax.rem(source - g - 1 + groups, groups)], gathered.at[source, eighth])
            for peer in peers:
                pltpu.make_async_remote_copy(
                    src_ref=gathered.at[source, piece], dst_ref=gathered.at[source, piece],
                    send_sem=sends, recv_sem=recvs, device_id=(peer, g), device_id_type=MESH,
                ).start()

    loads[1].wait()
    blocks = height // 2
    blank = jnp.zeros((3 * chans, chans), BF16)
    wide = jnp.concatenate(
        [
            jnp.concatenate([fine[ab * 3 + c] for c in range(3)], axis=1)
            for ab in range(9)
        ],
        axis=0,
    )
    both = split(wide.T)

    def taps_at(x, b):
        return [x[:, (a * 3 + b) * chans : (a * 3 + b + 1) * chans] for a in range(3)] if 0 <= b < 3 else [blank] * 3

    within = [[n for n in range(4) if 1 <= 2 * block + n <= height] for block in range(blocks)]
    beyond = [(0, 0, 0), (3, 1, 2)]
    for block in range(blocks):
        for hb in range(2):
            parts = []
            for x in both:
                by_line = [taps_at(x, n - hb) for n in within[block]]
                parts.append(jnp.concatenate([line[a] for a in range(3) for line in by_line], axis=1))
            inner[block, hb * 3 * chans : (hb + 1) * 3 * chans] = jnp.concatenate([parts[0], parts[1], parts[0]], axis=1)
    for k, (_, _, b) in enumerate(beyond):
        parts = [jnp.concatenate(taps_at(x, b), axis=1) for x in both]
        outer[k] = jnp.concatenate([parts[0], parts[1], parts[0]], axis=1)
    for n in range(1, rounds):
        vouch(n)
    d2, h2, c2 = depth // 2, blocks, down1.shape[2]
    for load in loads[2:5]:
        load.wait()
    for a in range(2):
        for b in range(2):
            for c in range(2):
                spot = pl.ds(((a * 2 + c) * 2 + b) * chans, chans)
                down1_w[spot, 0:c2], down1_w[spot, c2 : 2 * c2] = split(down1[a, (b * 2 + c) * chans : (b * 2 + c + 1) * chans])

    @pl.loop(0, 3)
    def _(a):
        for line in range(1, h2 + 1):
            rows = pl.ds(pl.multiple_of((a * h2 + line - 1) * c2, c2), c2)
            for hb in range(h2):
                for c in range(3):
                    columns = pl.ds((hb * 3 + c) * c2, c2)
                    if 0 <= line - hb < 3:
                        mid_h[rows, columns], mid_l[rows, columns] = split(middle[a * 3 + line - hb, c * c2 : (c + 1) * c2])
                    else:
                        mid_h[rows, columns] = mid_l[rows, columns] = jnp.zeros((c2, c2), BF16)
        rows = pl.ds(pl.multiple_of(a * c2, c2), c2)
        for k, b in ((0, 0), (1, 2)):
            for c in range(3):
                columns = pl.ds(c * c2, c2)
                side_h[k, rows, columns], side_l[k, rows, columns] = split(middle[a * 3 + b, c * c2 : (c + 1) * c2])

    outs = coarse_w.shape[2]
    c3 = coarse.shape[3]

    def prepare_coarse():
        loads[5].wait()

        @pl.loop(0, 3)
        def _(a):
            for b in range(3):
                for c in range(3):
                    high, low = split(coarse_w[a * 3 + b, c * c3 : (c + 1) * c3])
                    spot = (b * 3 + c) * outs
                    coarse_b[a, :, spot : spot + outs] = high
                    coarse_b[a, :, 9 * outs + spot : 10 * outs + spot] = low

    def narrow(ds, hs):
        field_h[ds, hs], field_l[ds, hs] = split(field[ds, hs])

    def across(first, count, d):
        columns = []
        for e in range(2):
            place = (pl.ds(d + e, 3), slice(first, first + count))
            high = field_h[place].reshape(3 * count * chans, width)
            low = field_l[place].reshape(3 * count * chans, width)
            columns.append(jnp.concatenate([high, high, low], axis=0))
        return jnp.concatenate(columns, axis=1)

    dot = functools.partial(jnp.dot, preferred_element_type=F32)
    narrow(slice(1, depth + 1), slice(1, height + 1))
    pairs = [jnp.where(parity == 0, d2 - 1, 0)] + list(range(1, d2 - 1))
    pairs.append(d2 - 1 - pairs[0])
    for n, k in enumerate(pairs):
        if n == d2 - 1:
            hand_on(eighth, load_sem.at[0], xrecv.at[0], crossings, True, (1,))
        if n in (0, d2 - 1):
            for way in range(2):
                mine = (parity == 1 - way) if n == 0 else (parity == way)

                @pl.when(mine)
                def _():
                    arrive(first, True, (way,))
            narrow(pl.ds(jnp.where(k == 0, 0, depth + 1), 1), slice(1, height + 1))
        for block in range(blocks):
            partial[block, k] = dot(inner[block], across(2 * block + within[block][0], len(within[block]), 2 * k))
    hand_on(eighth, load_sem.at[0], xrecv.at[0], crossings, True, range(2, groups))
    arrive(first, True, range(2, len(WAYS)))
    for h in (0, height + 1):
        narrow(slice(0, depth + 2), slice(h, h + 1))
    halves = []
    for block in range(blocks):
        n, extra_hb, _ = beyond[block]
        for k in range(d2):
            extra = dot(outer[block], across(2 * block + n, 1, 2 * k))
            row = []
            for e in range(2):
                ends = []
                for hb in range(2):
                    x = partial[block, k, hb * 3 * chans : (hb + 1) * 3 * chans, e * width : (e + 1) * width]
                    if hb == extra_hb:
                        x = x + extra[:, e * width : (e + 1) * width]
                    ends.append(apart(x, width, chans))
                spot = (block * d2 + k) * 2 + e
                turned[spot] = gelu(jnp.concatenate(ends, axis=0)).T
                row += [turned[spot, pl.ds(c, half, stride=2), :] for c in range(2)]
            halves.append(jnp.concatenate(row, axis=1))
    lhs = jnp.concatenate(halves, axis=0)
    wide = dot(stacked(lhs), down1_w[...])
    cells1 = lhs.shape[0]
    total = wide[:cells1, :c2] + wide[:cells1, c2:] + wide[cells1:, :c2]
    total = total.reshape(h2, d2, half, c2)
    for h in range(h2):
        second[1 : d2 + 1, 1 + h] = total[h]
    arrive(first, False)
    again = halo(second, 1, second, face_sem, recv2)
    prepare_coarse()
    def thin(h):
        spot = slice(h * c2, (h + 1) * c2)
        second_h[:, :, spot], second_l[:, :, spot] = split(second[:, h])

    def gathered_taps(low, high):
        parts = []
        for x in (second_h, second_l):
            parts.append(
                jnp.concatenate([x[a : a + d2, :, low:high].reshape(d2 * half, high - low) for a in range(3)], axis=1)
            )
        return jnp.concatenate(parts, axis=0)

    arrive(again, True, range(0, 2))
    for h in range(1, h2 + 1):
        thin(h)
    total = product(gathered_taps(c2, (1 + h2) * c2), (mid_h[...], mid_l[...]))
    settle(xrecv.at[0], gathered.at[foreign, 0 : 3 * (taps_of // 8)])
    hand_on(half_taps, load_sem.at[1], frecv.at[0], [sibling])
    arrive(again, True, range(2, len(WAYS)))
    for h in (0, h2 + 1):
        thin(h)
    sides = [
        product(gathered_taps(h * c2, (h + 1) * c2), (side_h[k], side_l[k])) for k, h in ((0, 0), (1, h2 + 1))
    ]
    for h in range(h2):
        x = total[:, h * 3 * c2 : (h + 1) * 3 * c2]
        if h == 0:
            x = x + sides[0]
        if h == h2 - 1:
            x = x + sides[1]
        before, _ = beside(x[:, :c2], half)
        _, after = beside(x[:, 2 * c2 :], half)
        level2[h] = gelu(before + x[:, c2 : 2 * c2] + after)
    quarter = half // 2
    lhs = jnp.concatenate(
        [
            level2[h, pl.ds(d * half + c, quarter, stride=2), :]
            for d in range(d2) for h in range(h2) for c in range(2)
        ],
        axis=1,
    )
    lhs = stacked(lhs)
    settle(frecv.at[0], gathered.at[foreign, 0 : taps_of // 2])
    filters = jnp.concatenate(
        [gathered[:, t].reshape(groups * shard.shape[1], c2) for t in range(taps_of)], axis=1
    )
    share = product(lhs, split(filters), (((1,), (1,)), ((), ())))
    coarse[1, pl.ds(g, 1)] = share[None]
    cells = groups * quarter

    def sideways(n):
        for k, ds in enumerate((1, -1)):
            copy = pltpu.make_async_remote_copy(
                src_ref=coarse.at[1, order[n]], dst_ref=coarse.at[1 - ds, order[n]],
                send_sem=load_sem.at[3 + k], recv_sem=nrecv.at[k, (n + 1) // 2],
                device_id=(s + ds, g), device_id_type=MESH,
            )

            @pl.when(exists(ds, 0))
            def _():
                copy.start()

    for n in range(groups - 1, 0, -1):
        pltpu.make_async_remote_copy(
            src_ref=coarse.at[1, g], dst_ref=coarse.at[1, g],
            send_sem=load_sem.at[2], recv_sem=crecv.at[lax.rem(g - order[n] - 1 + groups, groups)],
            device_id=(s, order[n]), device_id_type=MESH,
        ).start()
    sideways(0)

    def terms(ns, plane):
        x = jnp.concatenate([coarse[plane, pl.ds(order[n], 1)][0] for n in ns], axis=0)
        size = len(ns) * quarter
        wide = dot(stacked(x), coarse_b[plane])
        span = 9 * outs
        wide = wide[:size, :span] + wide[:size, span:] + wide[size:, :span]
        for k, n in enumerate(ns):
            for b in range(3):
                spot = pl.ds(pl.multiple_of((order[n] + 2 - b) * quarter, quarter), quarter)
                sums[spot] = sums[spot] + wide[k * quarter : (k + 1) * quarter, b * 3 * outs : (b + 1) * 3 * outs]

    def own(ns):
        for n in ns:
            if n:
                settle(crecv.at[lax.rem(order[n] - g - 1 + groups, groups)], coarse.at[1, order[n]])
                sideways(n)
        terms(ns, 1)

    def others(ns):
        for plane in (2 - 2 * parity, 2 * parity):

            @pl.when(exists(plane - 1, 0))
            def _():
                settle(nrecv.at[plane // 2, (ns[0] + 1) // 2], coarse.at[1, 0 : len(ns)])

            terms(ns, plane)

    for plane in (0, 2):
        @pl.when(jnp.logical_not(exists(plane - 1, 0)))
        def _():
            coarse[plane] = jnp.zeros(coarse.shape[1:], F32)

    sums[...] = jnp.zeros(sums.shape, F32)
    stages = [[0]] + [list(range(n, min(n + 2, groups))) for n in range(1, groups, 2)]
    for k, stage in enumerate(stages):
        own(stage)
        if 0 < k < len(stages) - 1:
            others(stages[k - 1])
    for stage in stages[-2:]:
        others(stage)
    x = sums[quarter : quarter + cells]
    before, _ = beside(x[:, :outs], quarter)
    _, after = beside(x[:, 2 * outs :], quarter)
    out[...] = gelu(before + x[:, outs : 2 * outs] + after).T

    arrive(again, False)
    settle(spread_sem.at[0], gathered.at[foreign, 0 : taps_of // 8])
    settle(load_sem.at[0], gathered.at[foreign, 0 : 3 * (taps_of // 8)])
    settle(load_sem.at[1], gathered.at[foreign, 0 : taps_of // 2])
    settle(load_sem.at[2], coarse.at[1, 0 : groups - 1])
    for k, ds in enumerate((1, -1)):
        @pl.when(exists(ds, 0))
        def _():
            settle(load_sem.at[3 + k], coarse.at[1])


def per_device(slabs, groups, volume, conv_fine, down_first, conv_middle, down_second, conv_coarse):
    c1, depth, height, width = volume.shape
    c2, c3, c4 = down_first.shape[4], conv_coarse.shape[3], conv_coarse.shape[4]
    half, quarter = width // 2, width // 4
    d2, h2 = depth // 2, height // 2
    part = down_second.shape[4]
    cells = groups * quarter
    vol = volume.reshape(c1 * depth * height, width)
    fine = conv_fine.reshape(27, c1, c1)
    down1 = down_first.reshape(2, 4 * c1, c2)
    middle = conv_middle.reshape(9, 3 * c2, c2)
    shard = jnp.swapaxes(down_second, 3, 4).reshape(8, part, c2)
    coarse_w = conv_coarse.reshape(9, 3 * c3, c4)
    V = pltpu.VMEM
    vmem, away = pl.BlockSpec(memory_space=pltpu.VMEM), pl.BlockSpec(memory_space=pl.ANY)
    dma = pltpu.SemaphoreType.DMA
    result = pl.pallas_call(
        functools.partial(kernel, slabs, groups),
        out_shape=pltpu.VMEM((c4, cells), F32),
        in_specs=[away] * 6,
        out_specs=vmem,
        scratch_shapes=[
            V(vol.shape, F32),
            V(fine.shape, F32),
            V((depth + 2, height + 2, c1, width), F32),
            V((depth + 2, height + 2, c1, width), BF16),
            V((depth + 2, height + 2, c1, width), BF16),
            V((2, 6 * c1, 27 * c1), BF16),
            V((2, 3 * c1, 9 * c1), BF16),
            V((2, d2, 6 * c1, 2 * width), F32),
            V((2 * d2 * 2, width, 2 * c1), F32),
            V(down1.shape, F32),
            V((8 * c1, 2 * c2), BF16),
            V(middle.shape, F32),
            V((3 * h2 * c2, 3 * h2 * c2), BF16),
            V((3 * h2 * c2, 3 * h2 * c2), BF16),
            V((2, 3 * c2, 3 * c2), BF16),
            V((2, 3 * c2, 3 * c2), BF16),
            V((d2 + 2, h2 + 2, half, c2), F32),
            V((d2 + 2, half, (h2 + 2) * c2), BF16),
            V((d2 + 2, half, (h2 + 2) * c2), BF16),
            V((h2, d2 * half, c2), F32),
            V((groups,) + shard.shape, F32),
            V(coarse_w.shape, F32),
            V((3, c3, 18 * c4), BF16),
            V((3, groups, quarter, c3), F32),
            V((cells + 2 * quarter, 3 * c4), F32),
            dma((6,)),
            pltpu.SemaphoreType.REGULAR((max(1, groups - 2),)),
            dma((8,)), dma((8,)), dma((8,)),
            dma((1,)), dma((groups - 1,)), dma((1,)), dma((1,)), dma((groups - 1,)), dma((2, 1 + groups // 2)),
        ],
        compiler_params=pltpu.CompilerParams(
            collective_id=0, has_side_effects=True, vmem_limit_bytes=60 * 1024 * 1024
        ),
    )(vol, fine, down1, middle, shard, coarse_w)
    return result.reshape(c4, 1, cells)


def solution(mesh):
    placed = (
        P(None, "slab", "grp", None),
        P(),
        P(),
        P(),
        P(None, None, None, None, "grp"),
        P(None, None, None, None, "grp"),
    )
    body = functools.partial(per_device, mesh.shape["slab"], mesh.shape["grp"])
    return jax.shard_map(
        body, mesh=mesh, in_specs=placed, out_specs=P("grp", "slab", None), check_vma=False
    )
```

```python
import functools

import jax
import jax.numpy as jnp
from jax import lax
from jax.experimental import pallas as pl
from jax.experimental.pallas import tpu as pltpu
from jax.sharding import PartitionSpec as P

MESH = pl.DeviceIdType.MESH
F32, BF16 = jnp.float32, jnp.bfloat16
WAYS = ((1, 0), (-1, 0), (0, 1), (0, -1), (1, 1), (1, -1), (-1, 1), (-1, -1))


def split(x):
    high = x.astype(BF16)
    return high, (x - high.astype(F32)).astype(BF16)


def stacked(x):
    return jnp.concatenate(split(x), axis=0)


def product(both, weights, dims=(((1,), (0,)), ((), ()))):
    dot = functools.partial(lax.dot_general, dimension_numbers=dims, preferred_element_type=F32)
    rows = both.shape[0] // 2
    wide = dot(both, weights[0])
    return wide[:rows] + wide[rows:] + dot(both[:rows], weights[1])


def plus(total, term):
    return term if total is None else total + term


def gelu(x):
    return 0.5 * x * (1.0 + lax.erf(x * (0.5**0.5)))


def apart(x, width, chans):
    lane = lax.broadcasted_iota(jnp.int32, (chans, width), 1)
    before = jnp.where(lane == 0, 0.0, pltpu.roll(x[:chans], 1, 1))
    after = jnp.where(lane == width - 1, 0.0, pltpu.roll(x[2 * chans :], width - 1, 1))
    return before + x[chans : 2 * chans] + after


def beside(x, span):
    at = lax.rem(lax.broadcasted_iota(jnp.int32, x.shape, 0), span)
    before = jnp.where(at == 0, 0.0, pltpu.roll(x, 1, 0))
    after = jnp.where(at == span - 1, 0.0, pltpu.roll(x, x.shape[0] - 1, 0))
    return before, after


def kernel(
    slabs, groups,
    vol_hbm, fine_hbm, down1_hbm, middle_hbm, shard, coarse_hbm,
    out,
    vol, fine, field, field_h, field_l, inner, outer, partial, turned, down1, down1_w, middle,
    mid_h, mid_l, side_h, side_l, second, second_h, second_l, level2, gathered, coarse_w, coarse_b,
    coarse, sums,
    load_sem, ready, face_sem, recv1, recv2, spread_sem, wrecv, xrecv, frecv, crecv, nrecv,
):
    s, g = lax.axis_index("slab"), lax.axis_index("grp")
    depth, height, chans, width = (field.shape[0] - 2, field.shape[1] - 2) + field.shape[2:]
    half = width // 2

    loads = [
        pltpu.make_async_copy(vol_hbm, vol, load_sem.at[3]),
        pltpu.make_async_copy(fine_hbm, fine, load_sem.at[4]),
        pltpu.make_async_copy(shard, gathered.at[g], load_sem.at[5]),
        pltpu.make_async_copy(down1_hbm, down1, load_sem.at[0]),
        pltpu.make_async_copy(middle_hbm, middle, load_sem.at[1]),
        pltpu.make_async_copy(coarse_hbm, coarse_w, load_sem.at[2]),
    ]
    for load in loads:
        load.start()

    def exists(ds, dg):
        return (s + ds >= 0) & (s + ds < slabs) & (g + dg >= 0) & (g + dg < groups)

    barrier = pltpu.get_barrier_semaphore()
    heard = jnp.int32(0)
    for ds, dg in WAYS[:4]:
        there = exists(ds, dg)
        heard = heard + there.astype(jnp.int32)

        @pl.when(there)
        def _():
            pl.semaphore_signal(barrier, inc=1, device_id=(s + ds, g + dg), device_id_type=MESH)

    sibling = s + 1 - 2 * lax.rem(s, 2)
    low, high = lax.rem(s // 2, 2), lax.rem(s // 4, 2)
    crossings = [s + 2 - 4 * low, s + 4 - 8 * high, s + 6 - 4 * low - 8 * high]
    for peer in crossings:
        pl.semaphore_signal(barrier, inc=1, device_id=(peer, g), device_id_type=MESH)
    pl.semaphore_wait(barrier, heard + len(crossings))

    taps_of = shard.shape[0]
    parity = lax.rem(s, 2)
    eighth = pl.ds((parity * 4 + lax.rem(s // 2, 4)) * (taps_of // 8), taps_of // 8)
    half_taps = pl.ds(parity * (taps_of // 2), taps_of // 2)
    def nth(n):
        spare = jnp.minimum(g, groups - 1 - g)
        near = (n + 1) // 2 if n % 2 else -(n // 2)
        away = jnp.where(2 * g < groups - 1, 1, -1)
        return g + jnp.where(n <= 2 * spare, near, away * (n - spare))

    order = [nth(n) for n in range(groups)]
    rounds = max(1, groups - 2)

    def settle(sem, view):
        pltpu.make_async_remote_copy(
            src_ref=view, dst_ref=view, send_sem=sem, recv_sem=sem, device_id=(s, g), device_id_type=MESH
        ).wait_recv()

    def spread_to(n, there=True):
        copy = pltpu.make_async_remote_copy(
            src_ref=shard.at[eighth], dst_ref=gathered.at[g, eighth],
            send_sem=spread_sem.at[0], recv_sem=wrecv.at[lax.rem(g - order[n] - 1 + groups, groups)],
            device_id=(s, order[n]), device_id_type=MESH,
        )

        @pl.when(there)
        def _():
            copy.start()

    def announce(n):
        for ds, dg in WAYS[:4] if n == 0 else WAYS[2:4]:
            @pl.when(exists(ds, dg))
            def _():
                pl.semaphore_signal(ready.at[n], inc=1, device_id=(s + ds, g + dg), device_id_type=MESH)

    def listen(n):
        count = jnp.int32(0)
        for ds, dg in WAYS[:4] if n == 0 else WAYS[2:4]:
            count = count + exists(ds, dg).astype(jnp.int32)
        pl.semaphore_wait(ready.at[n], count)

    announce(0)
    spread_to(1)
    inside = (g > 0) & (g < groups - 1)
    if groups > 2:
        spread_to(2, inside)

    loads[0].wait()
    lines = depth * height
    for r in range(lines):
        field[1 + r // height, 1 + r % height] = vol[pl.ds(r, chans, stride=lines), :]
    def part(way, size, offset):
        if way == 0:
            return pl.ds(offset, size)
        return pl.ds(offset + (size - 1 if way > 0 else 0), 1)

    def landing(way, size):
        if way == 0:
            return pl.ds(1, size)
        return pl.ds(0 if way > 0 else size + 1, 1)

    def halo(src, offset, buf, sends, recvs, between=None):
        nd, nh = buf.shape[0] - 2, buf.shape[1] - 2
        copies = []
        for k, (ds, dg) in enumerate(WAYS):
            if k == 4 and between is not None:
                between()
            copies.append(
                pltpu.make_async_remote_copy(
                    src_ref=src.at[part(ds, nd, offset), part(dg, nh, offset)],
                    dst_ref=buf.at[landing(ds, nd), landing(dg, nh)],
                    send_sem=sends.at[k],
                    recv_sem=recvs.at[k],
                    device_id=(s + ds, g + dg),
                    device_id_type=MESH,
                )
            )

            @pl.when(exists(ds, dg))
            def _():
                copies[k].start()

            @pl.when(jnp.logical_not(exists(-ds, -dg)))
            def _():
                piece = (landing(ds, nd), landing(dg, nh))
                shape = (piece[0].size, piece[1].size) + buf.shape[2:]
                buf[piece[0], piece[1]] = jnp.zeros(shape, F32)

        return copies

    def arrive(copies, received, ways=range(len(WAYS))):
        for k in ways:
            ds, dg = WAYS[k]
            if received:
                @pl.when(exists(-ds, -dg))
                def _():
                    copies[k].wait_recv()
            else:
                @pl.when(exists(ds, dg))
                def _():
                    copies[k].wait_send()

    def vouch(n):
        listen(n)
        if n + 1 < rounds:
            announce(n + 1)
        if n + 2 < groups:
            spread_to(n + 2, jnp.logical_not(inside) if n == 0 else True)

    first = halo(field, 1, field, face_sem, recv1, lambda: vouch(0))

    foreign = slice(0, groups - 1)

    def hand_on(piece, sends, recvs, peers, spread=False, ns=range(1, groups)):
        for n in ns:
            source = order[n]
            if spread:
                settle(wrecv.at[lax.rem(source - g - 1 + groups, groups)], gathered.at[source, eighth])
            for peer in peers:
                pltpu.make_async_remote_copy(
                    src_ref=gathered.at[source, piece], dst_ref=gathered.at[source, piece],
                    send_sem=sends, recv_sem=recvs, device_id=(peer, g), device_id_type=MESH,
                ).start()

    loads[1].wait()
    blocks = height // 2
    blank = jnp.zeros((3 * chans, chans), BF16)
    wide = jnp.concatenate(
        [
            jnp.concatenate([fine[ab * 3 + c] for c in range(3)], axis=1)
            for ab in range(9)
        ],
        axis=0,
    )
    both = split(wide.T)

    def taps_at(x, b):
        return [x[:, (a * 3 + b) * chans : (a * 3 + b + 1) * chans] for a in range(3)] if 0 <= b < 3 else [blank] * 3

    within = [[n for n in range(4) if 1 <= 2 * block + n <= height] for block in range(blocks)]
    beyond = [(0, 0, 0), (3, 1, 2)]
    for block in range(blocks):
        for hb in range(2):
            parts = []
            for x in both:
                by_line = [taps_at(x, n - hb) for n in within[block]]
                parts.append(jnp.concatenate([line[a] for a in range(3) for line in by_line], axis=1))
            inner[block, hb * 3 * chans : (hb + 1) * 3 * chans] = jnp.concatenate([parts[0], parts[1], parts[0]], axis=1)
    for k, (_, _, b) in enumerate(beyond):
        parts = [jnp.concatenate(taps_at(x, b), axis=1) for x in both]
        outer[k] = jnp.concatenate([parts[0], parts[1], parts[0]], axis=1)
    for n in range(1, rounds):
        vouch(n)
    d2, h2, c2 = depth // 2, blocks, down1.shape[2]
    for load in loads[2:5]:
        load.wait()
    for a in range(2):
        for b in range(2):
            for c in range(2):
                spot = pl.ds(((a * 2 + c) * 2 + b) * chans, chans)
                down1_w[spot, 0:c2], down1_w[spot, c2 : 2 * c2] = split(down1[a, (b * 2 + c) * chans : (b * 2 + c + 1) * chans])

    @pl.loop(0, 3)
    def _(a):
        for line in range(1, h2 + 1):
            rows = pl.ds(pl.multiple_of((a * h2 + line - 1) * c2, c2), c2)
            for hb in range(h2):
                for c in range(3):
                    columns = pl.ds((hb * 3 + c) * c2, c2)
                    if 0 <= line - hb < 3:
                        mid_h[rows, columns], mid_l[rows, columns] = split(middle[a * 3 + line - hb, c * c2 : (c + 1) * c2])
                    else:
                        mid_h[rows, columns] = mid_l[rows, columns] = jnp.zeros((c2, c2), BF16)
        rows = pl.ds(pl.multiple_of(a * c2, c2), c2)
        for k, b in ((0, 0), (1, 2)):
            for c in range(3):
                columns = pl.ds(c * c2, c2)
                side_h[k, rows, columns], side_l[k, rows, columns] = split(middle[a * 3 + b, c * c2 : (c + 1) * c2])

    outs = coarse_w.shape[2]
    c3 = coarse.shape[3]

    def prepare_coarse():
        loads[5].wait()

        @pl.loop(0, 3)
        def _(a):
            for b in range(3):
                for c in range(3):
                    high, low = split(coarse_w[a * 3 + b, c * c3 : (c + 1) * c3])
                    spot = (b * 3 + c) * outs
                    coarse_b[a, :, spot : spot + outs] = high
                    coarse_b[a, :, 9 * outs + spot : 10 * outs + spot] = low

    def narrow(ds, hs):
        field_h[ds, hs], field_l[ds, hs] = split(field[ds, hs])

    def across(first, count, d):
        columns = []
        for e in range(2):
            place = (pl.ds(d + e, 3), slice(first, first + count))
            high = field_h[place].reshape(3 * count * chans, width)
            low = field_l[place].reshape(3 * count * chans, width)
            columns.append(jnp.concatenate([high, high, low], axis=0))
        return jnp.concatenate(columns, axis=1)

    dot = functools.partial(jnp.dot, preferred_element_type=F32)
    narrow(slice(1, depth + 1), slice(1, height + 1))
    pairs = [jnp.where(parity == 0, d2 - 1, 0)] + list(range(1, d2 - 1))
    pairs.append(d2 - 1 - pairs[0])
    for n, k in enumerate(pairs):
        if n == d2 - 1:
            hand_on(eighth, load_sem.at[0], xrecv.at[0], crossings, True, (1,))
        if n in (0, d2 - 1):
            for way in range(2):
                mine = (parity == 1 - way) if n == 0 else (parity == way)

                @pl.when(mine)
                def _():
                    arrive(first, True, (way,))
            narrow(pl.ds(jnp.where(k == 0, 0, depth + 1), 1), slice(1, height + 1))
        for block in range(blocks):
            partial[block, k] = dot(inner[block], across(2 * block + within[block][0], len(within[block]), 2 * k))
    hand_on(eighth, load_sem.at[0], xrecv.at[0], crossings, True, range(2, groups))
    arrive(first, True, range(2, len(WAYS)))
    for h in (0, height + 1):
        narrow(slice(0, depth + 2), slice(h, h + 1))
    halves = []
    for block in range(blocks):
        n, extra_hb, _ = beyond[block]
        for k in range(d2):
            extra = dot(outer[block], across(2 * block + n, 1, 2 * k))
            row = []
            for e in range(2):
                ends = []
                for hb in range(2):
                    x = partial[block, k, hb * 3 * chans : (hb + 1) * 3 * chans, e * width : (e + 1) * width]
                    if hb == extra_hb:
                        x = x + extra[:, e * width : (e + 1) * width]
                    ends.append(apart(x, width, chans))
                spot = (block * d2 + k) * 2 + e
                turned[spot] = gelu(jnp.concatenate(ends, axis=0)).T
                row += [turned[spot, pl.ds(c, half, stride=2), :] for c in range(2)]
            halves.append(jnp.concatenate(row, axis=1))
    lhs = jnp.concatenate(halves, axis=0)
    wide = dot(stacked(lhs), down1_w[...])
    cells1 = lhs.shape[0]
    total = wide[:cells1, :c2] + wide[:cells1, c2:] + wide[cells1:, :c2]
    total = total.reshape(h2, d2, half, c2)
    for h in range(h2):
        second[1 : d2 + 1, 1 + h] = total[h]
    arrive(first, False)
    again = halo(second, 1, second, face_sem, recv2)
    prepare_coarse()
    def thin(h):
        spot = slice(h * c2, (h + 1) * c2)
        second_h[:, :, spot], second_l[:, :, spot] = split(second[:, h])

    def gathered_taps(low, high):
        parts = []
        for x in (second_h, second_l):
            parts.append(
                jnp.concatenate([x[a : a + d2, :, low:high].reshape(d2 * half, high - low) for a in range(3)], axis=1)
            )
        return jnp.concatenate(parts, axis=0)

    settle(xrecv.at[0], gathered.at[foreign, 0 : 3 * (taps_of // 8)])
    hand_on(half_taps, load_sem.at[1], frecv.at[0], [sibling])
    arrive(again, True, range(0, 2))
    for h in range(1, h2 + 1):
        thin(h)
    total = product(gathered_taps(c2, (1 + h2) * c2), (mid_h[...], mid_l[...]))
    arrive(again, True, range(2, len(WAYS)))
    for h in (0, h2 + 1):
        thin(h)
    sides = [
        product(gathered_taps(h * c2, (h + 1) * c2), (side_h[k], side_l[k])) for k, h in ((0, 0), (1, h2 + 1))
    ]
    for h in range(h2):
        x = total[:, h * 3 * c2 : (h + 1) * 3 * c2]
        if h == 0:
            x = x + sides[0]
        if h == h2 - 1:
            x = x + sides[1]
        before, _ = beside(x[:, :c2], half)
        _, after = beside(x[:, 2 * c2 :], half)
        level2[h] = gelu(before + x[:, c2 : 2 * c2] + after)
    quarter = half // 2
    lhs = jnp.concatenate(
        [
            level2[h, pl.ds(d * half + c, quarter, stride=2), :]
            for d in range(d2) for h in range(h2) for c in range(2)
        ],
        axis=1,
    )
    lhs = stacked(lhs)
    settle(frecv.at[0], gathered.at[foreign, 0 : taps_of // 2])
    filters = jnp.concatenate(
        [gathered[:, t].reshape(groups * shard.shape[1], c2) for t in range(taps_of)], axis=1
    )
    share = product(lhs, split(filters), (((1,), (1,)), ((), ())))
    coarse[1, pl.ds(g, 1)] = share[None]
    cells = groups * quarter

    def sideways(n):
        for k, ds in enumerate((1, -1)):
            copy = pltpu.make_async_remote_copy(
                src_ref=coarse.at[1, order[n]], dst_ref=coarse.at[1 - ds, order[n]],
                send_sem=load_sem.at[3 + k], recv_sem=nrecv.at[k, (n + 1) // 2],
                device_id=(s + ds, g), device_id_type=MESH,
            )

            @pl.when(exists(ds, 0))
            def _():
                copy.start()

    for n in range(groups - 1, 0, -1):
        pltpu.make_async_remote_copy(
            src_ref=coarse.at[1, g], dst_ref=coarse.at[1, g],
            send_sem=load_sem.at[2], recv_sem=crecv.at[lax.rem(g - order[n] - 1 + groups, groups)],
            device_id=(s, order[n]), device_id_type=MESH,
        ).start()
    sideways(0)

    def terms(ns, plane):
        x = jnp.concatenate([coarse[plane, pl.ds(order[n], 1)][0] for n in ns], axis=0)
        size = len(ns) * quarter
        wide = dot(stacked(x), coarse_b[plane])
        span = 9 * outs
        wide = wide[:size, :span] + wide[:size, span:] + wide[size:, :span]
        for k, n in enumerate(ns):
            for b in range(3):
                spot = pl.ds(pl.multiple_of((order[n] + 2 - b) * quarter, quarter), quarter)
                sums[spot] = sums[spot] + wide[k * quarter : (k + 1) * quarter, b * 3 * outs : (b + 1) * 3 * outs]

    def own(ns):
        for n in ns:
            if n:
                settle(crecv.at[lax.rem(order[n] - g - 1 + groups, groups)], coarse.at[1, order[n]])
                sideways(n)
        terms(ns, 1)

    def others(ns):
        for plane in (2 - 2 * parity, 2 * parity):

            @pl.when(exists(plane - 1, 0))
            def _():
                settle(nrecv.at[plane // 2, (ns[0] + 1) // 2], coarse.at[1, 0 : len(ns)])

            terms(ns, plane)

    for plane in (0, 2):
        @pl.when(jnp.logical_not(exists(plane - 1, 0)))
        def _():
            coarse[plane] = jnp.zeros(coarse.shape[1:], F32)

    sums[...] = jnp.zeros(sums.shape, F32)
    stages = [[0]] + [list(range(n, min(n + 2, groups))) for n in range(1, groups, 2)]
    for k, stage in enumerate(stages):
        own(stage)
        if 0 < k < len(stages) - 2:
            others(stages[k - 1])
    for stage in stages[max(0, len(stages) - 3) :]:
        others(stage)
    x = sums[quarter : quarter + cells]
    before, _ = beside(x[:, :outs], quarter)
    _, after = beside(x[:, 2 * outs :], quarter)
    out[...] = gelu(before + x[:, outs : 2 * outs] + after).T

    arrive(again, False)
    settle(spread_sem.at[0], gathered.at[foreign, 0 : taps_of // 8])
    settle(load_sem.at[0], gathered.at[foreign, 0 : 3 * (taps_of // 8)])
    settle(load_sem.at[1], gathered.at[foreign, 0 : taps_of // 2])
    settle(load_sem.at[2], coarse.at[1, 0 : groups - 1])
    for k, ds in enumerate((1, -1)):
        @pl.when(exists(ds, 0))
        def _():
            settle(load_sem.at[3 + k], coarse.at[1])


def per_device(slabs, groups, volume, conv_fine, down_first, conv_middle, down_second, conv_coarse):
    c1, depth, height, width = volume.shape
    c2, c3, c4 = down_first.shape[4], conv_coarse.shape[3], conv_coarse.shape[4]
    half, quarter = width // 2, width // 4
    d2, h2 = depth // 2, height // 2
    part = down_second.shape[4]
    cells = groups * quarter
    vol = volume.reshape(c1 * depth * height, width)
    fine = conv_fine.reshape(27, c1, c1)
    down1 = down_first.reshape(2, 4 * c1, c2)
    middle = conv_middle.reshape(9, 3 * c2, c2)
    shard = jnp.swapaxes(down_second, 3, 4).reshape(8, part, c2)
    coarse_w = conv_coarse.reshape(9, 3 * c3, c4)
    V = pltpu.VMEM
    vmem, away = pl.BlockSpec(memory_space=pltpu.VMEM), pl.BlockSpec(memory_space=pl.ANY)
    dma = pltpu.SemaphoreType.DMA
    result = pl.pallas_call(
        functools.partial(kernel, slabs, groups),
        out_shape=pltpu.VMEM((c4, cells), F32),
        in_specs=[away] * 6,
        out_specs=vmem,
        scratch_shapes=[
            V(vol.shape, F32),
            V(fine.shape, F32),
            V((depth + 2, height + 2, c1, width), F32),
            V((depth + 2, height + 2, c1, width), BF16),
            V((depth + 2, height + 2, c1, width), BF16),
            V((2, 6 * c1, 27 * c1), BF16),
            V((2, 3 * c1, 9 * c1), BF16),
            V((2, d2, 6 * c1, 2 * width), F32),
            V((2 * d2 * 2, width, 2 * c1), F32),
            V(down1.shape, F32),
            V((8 * c1, 2 * c2), BF16),
            V(middle.shape, F32),
            V((3 * h2 * c2, 3 * h2 * c2), BF16),
            V((3 * h2 * c2, 3 * h2 * c2), BF16),
            V((2, 3 * c2, 3 * c2), BF16),
            V((2, 3 * c2, 3 * c2), BF16),
            V((d2 + 2, h2 + 2, half, c2), F32),
            V((d2 + 2, half, (h2 + 2) * c2), BF16),
            V((d2 + 2, half, (h2 + 2) * c2), BF16),
            V((h2, d2 * half, c2), F32),
            V((groups,) + shard.shape, F32),
            V(coarse_w.shape, F32),
            V((3, c3, 18 * c4), BF16),
            V((3, groups, quarter, c3), F32),
            V((cells + 2 * quarter, 3 * c4), F32),
            dma((6,)),
            pltpu.SemaphoreType.REGULAR((max(1, groups - 2),)),
            dma((8,)), dma((8,)), dma((8,)),
            dma((1,)), dma((groups - 1,)), dma((1,)), dma((1,)), dma((groups - 1,)), dma((2, 1 + groups // 2)),
        ],
        compiler_params=pltpu.CompilerParams(
            collective_id=0, has_side_effects=True, vmem_limit_bytes=60 * 1024 * 1024
        ),
    )(vol, fine, down1, middle, shard, coarse_w)
    return result.reshape(c4, 1, cells)


def solution(mesh):
    placed = (
        P(None, "slab", "grp", None),
        P(),
        P(),
        P(),
        P(None, None, None, None, "grp"),
        P(None, None, None, None, "grp"),
    )
    body = functools.partial(per_device, mesh.shape["slab"], mesh.shape["grp"])
    return jax.shard_map(
        body, mesh=mesh, in_specs=placed, out_specs=P("grp", "slab", None), check_vma=False
    )
```

```python
import functools

import jax
import jax.numpy as jnp
from jax import lax
from jax.experimental import pallas as pl
from jax.experimental.pallas import tpu as pltpu
from jax.sharding import PartitionSpec as P

MESH = pl.DeviceIdType.MESH
F32, BF16 = jnp.float32, jnp.bfloat16
WAYS = ((1, 0), (-1, 0), (0, 1), (0, -1), (1, 1), (1, -1), (-1, 1), (-1, -1))


def split(x):
    high = x.astype(BF16)
    return high, (x - high.astype(F32)).astype(BF16)


def stacked(x):
    return jnp.concatenate(split(x), axis=0)


def product(both, weights, dims=(((1,), (0,)), ((), ()))):
    dot = functools.partial(lax.dot_general, dimension_numbers=dims, preferred_element_type=F32)
    rows = both.shape[0] // 2
    wide = dot(both, weights[0])
    return wide[:rows] + wide[rows:] + dot(both[:rows], weights[1])


def plus(total, term):
    return term if total is None else total + term


def gelu(x):
    return 0.5 * x * (1.0 + lax.erf(x * (0.5**0.5)))


def apart(x, width, chans):
    lane = lax.broadcasted_iota(jnp.int32, (chans, width), 1)
    before = jnp.where(lane == 0, 0.0, pltpu.roll(x[:chans], 1, 1))
    after = jnp.where(lane == width - 1, 0.0, pltpu.roll(x[2 * chans :], width - 1, 1))
    return before + x[chans : 2 * chans] + after


def beside(x, span):
    at = lax.rem(lax.broadcasted_iota(jnp.int32, x.shape, 0), span)
    before = jnp.where(at == 0, 0.0, pltpu.roll(x, 1, 0))
    after = jnp.where(at == span - 1, 0.0, pltpu.roll(x, x.shape[0] - 1, 0))
    return before, after


def kernel(
    slabs, groups,
    vol_hbm, fine_hbm, down1_hbm, middle_hbm, shard, coarse_hbm,
    out,
    vol, fine, field, field_h, field_l, inner, outer, partial, turned, down1, down1_w, middle,
    mid_h, mid_l, side_h, side_l, second, second_h, second_l, level2, gathered, coarse_w, coarse_b,
    coarse, sums,
    load_sem, ready, face_sem, recv1, recv2, spread_sem, wrecv, xrecv, frecv, crecv, nrecv,
):
    s, g = lax.axis_index("slab"), lax.axis_index("grp")
    depth, height, chans, width = (field.shape[0] - 2, field.shape[1] - 2) + field.shape[2:]
    half = width // 2

    loads = [
        pltpu.make_async_copy(vol_hbm, vol, load_sem.at[3]),
        pltpu.make_async_copy(fine_hbm, fine, load_sem.at[4]),
        pltpu.make_async_copy(shard, gathered.at[g], load_sem.at[5]),
        pltpu.make_async_copy(down1_hbm, down1, load_sem.at[0]),
        pltpu.make_async_copy(middle_hbm, middle, load_sem.at[1]),
        pltpu.make_async_copy(coarse_hbm, coarse_w, load_sem.at[2]),
    ]
    for load in loads:
        load.start()

    def exists(ds, dg):
        return (s + ds >= 0) & (s + ds < slabs) & (g + dg >= 0) & (g + dg < groups)

    barrier = pltpu.get_barrier_semaphore()
    heard = jnp.int32(0)
    for ds, dg in WAYS[:4]:
        there = exists(ds, dg)
        heard = heard + there.astype(jnp.int32)

        @pl.when(there)
        def _():
            pl.semaphore_signal(barrier, inc=1, device_id=(s + ds, g + dg), device_id_type=MESH)

    sibling = s + 1 - 2 * lax.rem(s, 2)
    low, high = lax.rem(s // 2, 2), lax.rem(s // 4, 2)
    crossings = [s + 2 - 4 * low, s + 4 - 8 * high, s + 6 - 4 * low - 8 * high]
    for peer in crossings:
        pl.semaphore_signal(barrier, inc=1, device_id=(peer, g), device_id_type=MESH)
    pl.semaphore_wait(barrier, heard + len(crossings))

    taps_of = shard.shape[0]
    parity = lax.rem(s, 2)
    eighth = pl.ds((parity * 4 + lax.rem(s // 2, 4)) * (taps_of // 8), taps_of // 8)
    half_taps = pl.ds(parity * (taps_of // 2), taps_of // 2)
    def nth(n):
        spare = jnp.minimum(g, groups - 1 - g)
        near = (n + 1) // 2 if n % 2 else -(n // 2)
        away = jnp.where(2 * g < groups - 1, 1, -1)
        return g + jnp.where(n <= 2 * spare, near, away * (n - spare))

    order = [nth(n) for n in range(groups)]
    rounds = max(1, groups - 2)

    def settle(sem, view):
        pltpu.make_async_remote_copy(
            src_ref=view, dst_ref=view, send_sem=sem, recv_sem=sem, device_id=(s, g), device_id_type=MESH
        ).wait_recv()

    def spread_to(n, there=True):
        copy = pltpu.make_async_remote_copy(
            src_ref=shard.at[eighth], dst_ref=gathered.at[g, eighth],
            send_sem=spread_sem.at[0], recv_sem=wrecv.at[lax.rem(g - order[n] - 1 + groups, groups)],
            device_id=(s, order[n]), device_id_type=MESH,
        )

        @pl.when(there)
        def _():
            copy.start()

    def announce(n):
        for ds, dg in WAYS[:4] if n == 0 else WAYS[2:4]:
            @pl.when(exists(ds, dg))
            def _():
                pl.semaphore_signal(ready.at[n], inc=1, device_id=(s + ds, g + dg), device_id_type=MESH)

    def listen(n):
        count = jnp.int32(0)
        for ds, dg in WAYS[:4] if n == 0 else WAYS[2:4]:
            count = count + exists(ds, dg).astype(jnp.int32)
        pl.semaphore_wait(ready.at[n], count)

    announce(0)
    spread_to(1)
    inside = (g > 0) & (g < groups - 1)
    if groups > 2:
        spread_to(2, inside)

    loads[0].wait()
    lines = depth * height
    for r in range(lines):
        field[1 + r // height, 1 + r % height] = vol[pl.ds(r, chans, stride=lines), :]
    def part(way, size, offset):
        if way == 0:
            return pl.ds(offset, size)
        return pl.ds(offset + (size - 1 if way > 0 else 0), 1)

    def landing(way, size):
        if way == 0:
            return pl.ds(1, size)
        return pl.ds(0 if way > 0 else size + 1, 1)

    def halo(src, offset, buf, sends, recvs, between=None):
        nd, nh = buf.shape[0] - 2, buf.shape[1] - 2
        copies = []
        for k, (ds, dg) in enumerate(WAYS):
            if k == 4 and between is not None:
                between()
            copies.append(
                pltpu.make_async_remote_copy(
                    src_ref=src.at[part(ds, nd, offset), part(dg, nh, offset)],
                    dst_ref=buf.at[landing(ds, nd), landing(dg, nh)],
                    send_sem=sends.at[k],
                    recv_sem=recvs.at[k],
                    device_id=(s + ds, g + dg),
                    device_id_type=MESH,
                )
            )

            @pl.when(exists(ds, dg))
            def _():
                copies[k].start()

            @pl.when(jnp.logical_not(exists(-ds, -dg)))
            def _():
                piece = (landing(ds, nd), landing(dg, nh))
                shape = (piece[0].size, piece[1].size) + buf.shape[2:]
                buf[piece[0], piece[1]] = jnp.zeros(shape, F32)

        return copies

    def arrive(copies, received, ways=range(len(WAYS))):
        for k in ways:
            ds, dg = WAYS[k]
            if received:
                @pl.when(exists(-ds, -dg))
                def _():
                    copies[k].wait_recv()
            else:
                @pl.when(exists(ds, dg))
                def _():
                    copies[k].wait_send()

    def vouch(n):
        listen(n)
        if n + 1 < rounds:
            announce(n + 1)
        if n + 2 < groups:
            spread_to(n + 2, jnp.logical_not(inside) if n == 0 else True)

    first = halo(field, 1, field, face_sem, recv1, lambda: vouch(0))

    foreign = slice(0, groups - 1)

    def hand_on(piece, sends, recvs, peers, spread=False, ns=range(1, groups)):
        for n in ns:
            source = order[n]
            if spread:
                settle(wrecv.at[lax.rem(source - g - 1 + groups, groups)], gathered.at[source, eighth])
            for peer in peers:
                pltpu.make_async_remote_copy(
                    src_ref=gathered.at[source, piece], dst_ref=gathered.at[source, piece],
                    send_sem=sends, recv_sem=recvs, device_id=(peer, g), device_id_type=MESH,
                ).start()

    loads[1].wait()
    blocks = height // 2
    blank = jnp.zeros((3 * chans, chans), BF16)
    wide = jnp.concatenate(
        [
            jnp.concatenate([fine[ab * 3 + c] for c in range(3)], axis=1)
            for ab in range(9)
        ],
        axis=0,
    )
    both = split(wide.T)

    def taps_at(x, b):
        return [x[:, (a * 3 + b) * chans : (a * 3 + b + 1) * chans] for a in range(3)] if 0 <= b < 3 else [blank] * 3

    within = [[n for n in range(4) if 1 <= 2 * block + n <= height] for block in range(blocks)]
    beyond = [(0, 0, 0), (3, 1, 2)]
    for block in range(blocks):
        for hb in range(2):
            parts = []
            for x in both:
                by_line = [taps_at(x, n - hb) for n in within[block]]
                parts.append(jnp.concatenate([line[a] for a in range(3) for line in by_line], axis=1))
            inner[block, hb * 3 * chans : (hb + 1) * 3 * chans] = jnp.concatenate([parts[0], parts[1], parts[0]], axis=1)
    for k, (_, _, b) in enumerate(beyond):
        parts = [jnp.concatenate(taps_at(x, b), axis=1) for x in both]
        outer[k] = jnp.concatenate([parts[0], parts[1], parts[0]], axis=1)
    for n in range(1, rounds):
        vouch(n)
    d2, h2, c2 = depth // 2, blocks, down1.shape[2]
    for load in loads[2:5]:
        load.wait()
    for a in range(2):
        for b in range(2):
            for c in range(2):
                spot = pl.ds(((a * 2 + c) * 2 + b) * chans, chans)
                down1_w[spot, 0:c2], down1_w[spot, c2 : 2 * c2] = split(down1[a, (b * 2 + c) * chans : (b * 2 + c + 1) * chans])

    @pl.loop(0, 3)
    def _(a):
        for line in range(1, h2 + 1):
            rows = pl.ds(pl.multiple_of((a * h2 + line - 1) * c2, c2), c2)
            for hb in range(h2):
                for c in range(3):
                    columns = pl.ds((hb * 3 + c) * c2, c2)
                    if 0 <= line - hb < 3:
                        mid_h[rows, columns], mid_l[rows, columns] = split(middle[a * 3 + line - hb, c * c2 : (c + 1) * c2])
                    else:
                        mid_h[rows, columns] = mid_l[rows, columns] = jnp.zeros((c2, c2), BF16)
        rows = pl.ds(pl.multiple_of(a * c2, c2), c2)
        for k, b in ((0, 0), (1, 2)):
            for c in range(3):
                columns = pl.ds(c * c2, c2)
                side_h[k, rows, columns], side_l[k, rows, columns] = split(middle[a * 3 + b, c * c2 : (c + 1) * c2])

    outs = coarse_w.shape[2]
    c3 = coarse.shape[3]

    def prepare_coarse():
        loads[5].wait()

        @pl.loop(0, 3)
        def _(a):
            for b in range(3):
                for c in range(3):
                    high, low = split(coarse_w[a * 3 + b, c * c3 : (c + 1) * c3])
                    spot = (b * 3 + c) * outs
                    coarse_b[a, :, spot : spot + outs] = high
                    coarse_b[a, :, 9 * outs + spot : 10 * outs + spot] = low

    def narrow(ds, hs):
        field_h[ds, hs], field_l[ds, hs] = split(field[ds, hs])

    def across(first, count, d):
        columns = []
        for e in range(2):
            place = (pl.ds(d + e, 3), slice(first, first + count))
            high = field_h[place].reshape(3 * count * chans, width)
            low = field_l[place].reshape(3 * count * chans, width)
            columns.append(jnp.concatenate([high, high, low], axis=0))
        return jnp.concatenate(columns, axis=1)

    dot = functools.partial(jnp.dot, preferred_element_type=F32)
    narrow(slice(1, depth + 1), slice(1, height + 1))
    pairs = [jnp.where(parity == 0, d2 - 1, 0)] + list(range(1, d2 - 1))
    pairs.append(d2 - 1 - pairs[0])
    for n, k in enumerate(pairs):
        if n == d2 - 1:
            hand_on(eighth, load_sem.at[0], xrecv.at[0], crossings, True, (1,))
        if n in (0, d2 - 1):
            for way in range(2):
                mine = (parity == 1 - way) if n == 0 else (parity == way)

                @pl.when(mine)
                def _():
                    arrive(first, True, (way,))
            narrow(pl.ds(jnp.where(k == 0, 0, depth + 1), 1), slice(1, height + 1))
        for block in range(blocks):
            partial[block, k] = dot(inner[block], across(2 * block + within[block][0], len(within[block]), 2 * k))
    hand_on(eighth, load_sem.at[0], xrecv.at[0], crossings, True, range(2, groups))
    arrive(first, True, range(2, len(WAYS)))
    for h in (0, height + 1):
        narrow(slice(0, depth + 2), slice(h, h + 1))
    halves = []
    for block in range(blocks):
        n, extra_hb, _ = beyond[block]
        for k in range(d2):
            extra = dot(outer[block], across(2 * block + n, 1, 2 * k))
            row = []
            for e in range(2):
                ends = []
                for hb in range(2):
                    x = partial[block, k, hb * 3 * chans : (hb + 1) * 3 * chans, e * width : (e + 1) * width]
                    if hb == extra_hb:
                        x = x + extra[:, e * width : (e + 1) * width]
                    ends.append(apart(x, width, chans))
                spot = (block * d2 + k) * 2 + e
                turned[spot] = gelu(jnp.concatenate(ends, axis=0)).T
                row += [turned[spot, pl.ds(c, half, stride=2), :] for c in range(2)]
            halves.append(jnp.concatenate(row, axis=1))
    lhs = jnp.concatenate(halves, axis=0)
    wide = dot(stacked(lhs), down1_w[...])
    cells1 = lhs.shape[0]
    total = wide[:cells1, :c2] + wide[:cells1, c2:] + wide[cells1:, :c2]
    total = total.reshape(h2, d2, half, c2)
    for h in range(h2):
        second[1 : d2 + 1, 1 + h] = total[h]
    arrive(first, False)
    again = halo(second, 1, second, face_sem, recv2)
    prepare_coarse()
    def thin(h):
        spot = slice(h * c2, (h + 1) * c2)
        second_h[:, :, spot], second_l[:, :, spot] = split(second[:, h])

    def gathered_taps(low, high):
        parts = []
        for x in (second_h, second_l):
            parts.append(
                jnp.concatenate([x[a : a + d2, :, low:high].reshape(d2 * half, high - low) for a in range(3)], axis=1)
            )
        return jnp.concatenate(parts, axis=0)

    settle(xrecv.at[0], gathered.at[foreign, 0 : 3 * (taps_of // 8)])
    hand_on(half_taps, load_sem.at[1], frecv.at[0], [sibling])
    arrive(again, True, range(0, 2))
    for h in range(1, h2 + 1):
        thin(h)
    total = product(gathered_taps(c2, (1 + h2) * c2), (mid_h[...], mid_l[...]))
    arrive(again, True, range(2, len(WAYS)))
    for h in (0, h2 + 1):
        thin(h)
    sides = [
        product(gathered_taps(h * c2, (h + 1) * c2), (side_h[k], side_l[k])) for k, h in ((0, 0), (1, h2 + 1))
    ]
    for h in range(h2):
        x = total[:, h * 3 * c2 : (h + 1) * 3 * c2]
        if h == 0:
            x = x + sides[0]
        if h == h2 - 1:
            x = x + sides[1]
        before, _ = beside(x[:, :c2], half)
        _, after = beside(x[:, 2 * c2 :], half)
        level2[h] = gelu(before + x[:, c2 : 2 * c2] + after)
    quarter = half // 2
    lhs = jnp.concatenate(
        [
            level2[h, pl.ds(d * half + c, quarter, stride=2), :]
            for d in range(d2) for h in range(h2) for c in range(2)
        ],
        axis=1,
    )
    lhs = stacked(lhs)
    settle(frecv.at[0], gathered.at[foreign, 0 : taps_of // 2])
    filters = jnp.concatenate(
        [gathered[:, t].reshape(groups * shard.shape[1], c2) for t in range(taps_of)], axis=1
    )
    share = product(lhs, split(filters), (((1,), (1,)), ((), ())))
    coarse[1, pl.ds(g, 1)] = share[None]
    cells = groups * quarter

    def sideways(n):
        for k, ds in enumerate((1, -1)):
            copy = pltpu.make_async_remote_copy(
                src_ref=coarse.at[1, order[n]], dst_ref=coarse.at[1 - ds, order[n]],
                send_sem=load_sem.at[3 + k], recv_sem=nrecv.at[k, (n + 1) // 2],
                device_id=(s + ds, g), device_id_type=MESH,
            )

            @pl.when(exists(ds, 0))
            def _():
                copy.start()

    for n in range(groups - 1, 0, -1):
        pltpu.make_async_remote_copy(
            src_ref=coarse.at[1, g], dst_ref=coarse.at[1, g],
            send_sem=load_sem.at[2], recv_sem=crecv.at[lax.rem(g - order[n] - 1 + groups, groups)],
            device_id=(s, order[n]), device_id_type=MESH,
        ).start()
    sideways(0)

    def terms(ns, plane):
        x = jnp.concatenate([coarse[plane, pl.ds(order[n], 1)][0] for n in ns], axis=0)
        size = len(ns) * quarter
        wide = dot(stacked(x), coarse_b[plane])
        span = 9 * outs
        wide = wide[:size, :span] + wide[:size, span:] + wide[size:, :span]
        for k, n in enumerate(ns):
            for b in range(3):
                spot = pl.ds(pl.multiple_of((order[n] + 2 - b) * quarter, quarter), quarter)
                sums[spot] = sums[spot] + wide[k * quarter : (k + 1) * quarter, b * 3 * outs : (b + 1) * 3 * outs]

    def own(ns):
        for n in ns:
            if n:
                settle(crecv.at[lax.rem(order[n] - g - 1 + groups, groups)], coarse.at[1, order[n]])
                sideways(n)
        terms(ns, 1)

    def others(ns):
        for plane in (2 - 2 * parity, 2 * parity):

            @pl.when(exists(plane - 1, 0))
            def _():
                settle(nrecv.at[plane // 2, (ns[0] + 1) // 2], coarse.at[1, 0 : len(ns)])

            terms(ns, plane)

    for plane in (0, 2):
        @pl.when(jnp.logical_not(exists(plane - 1, 0)))
        def _():
            coarse[plane] = jnp.zeros(coarse.shape[1:], F32)

    sums[...] = jnp.zeros(sums.shape, F32)
    stages = [[0]] + [list(range(n, min(n + 2, groups))) for n in range(1, groups, 2)]
    own(stages[0])
    own(list(range(1, groups)))
    for stage in stages[: max(0, len(stages) - 3)]:
        others(stage)
    for stage in stages[max(0, len(stages) - 3) :]:
        others(stage)
    x = sums[quarter : quarter + cells]
    before, _ = beside(x[:, :outs], quarter)
    _, after = beside(x[:, 2 * outs :], quarter)
    out[...] = gelu(before + x[:, outs : 2 * outs] + after).T

    arrive(again, False)
    settle(spread_sem.at[0], gathered.at[foreign, 0 : taps_of // 8])
    settle(load_sem.at[0], gathered.at[foreign, 0 : 3 * (taps_of // 8)])
    settle(load_sem.at[1], gathered.at[foreign, 0 : taps_of // 2])
    settle(load_sem.at[2], coarse.at[1, 0 : groups - 1])
    for k, ds in enumerate((1, -1)):
        @pl.when(exists(ds, 0))
        def _():
            settle(load_sem.at[3 + k], coarse.at[1])


def per_device(slabs, groups, volume, conv_fine, down_first, conv_middle, down_second, conv_coarse):
    c1, depth, height, width = volume.shape
    c2, c3, c4 = down_first.shape[4], conv_coarse.shape[3], conv_coarse.shape[4]
    half, quarter = width // 2, width // 4
    d2, h2 = depth // 2, height // 2
    part = down_second.shape[4]
    cells = groups * quarter
    vol = volume.reshape(c1 * depth * height, width)
    fine = conv_fine.reshape(27, c1, c1)
    down1 = down_first.reshape(2, 4 * c1, c2)
    middle = conv_middle.reshape(9, 3 * c2, c2)
    shard = jnp.swapaxes(down_second, 3, 4).reshape(8, part, c2)
    coarse_w = conv_coarse.reshape(9, 3 * c3, c4)
    V = pltpu.VMEM
    vmem, away = pl.BlockSpec(memory_space=pltpu.VMEM), pl.BlockSpec(memory_space=pl.ANY)
    dma = pltpu.SemaphoreType.DMA
    result = pl.pallas_call(
        functools.partial(kernel, slabs, groups),
        out_shape=pltpu.VMEM((c4, cells), F32),
        in_specs=[away] * 6,
        out_specs=vmem,
        scratch_shapes=[
            V(vol.shape, F32),
            V(fine.shape, F32),
            V((depth + 2, height + 2, c1, width), F32),
            V((depth + 2, height + 2, c1, width), BF16),
            V((depth + 2, height + 2, c1, width), BF16),
            V((2, 6 * c1, 27 * c1), BF16),
            V((2, 3 * c1, 9 * c1), BF16),
            V((2, d2, 6 * c1, 2 * width), F32),
            V((2 * d2 * 2, width, 2 * c1), F32),
            V(down1.shape, F32),
            V((8 * c1, 2 * c2), BF16),
            V(middle.shape, F32),
            V((3 * h2 * c2, 3 * h2 * c2), BF16),
            V((3 * h2 * c2, 3 * h2 * c2), BF16),
            V((2, 3 * c2, 3 * c2), BF16),
            V((2, 3 * c2, 3 * c2), BF16),
            V((d2 + 2, h2 + 2, half, c2), F32),
            V((d2 + 2, half, (h2 + 2) * c2), BF16),
            V((d2 + 2, half, (h2 + 2) * c2), BF16),
            V((h2, d2 * half, c2), F32),
            V((groups,) + shard.shape, F32),
            V(coarse_w.shape, F32),
            V((3, c3, 18 * c4), BF16),
            V((3, groups, quarter, c3), F32),
            V((cells + 2 * quarter, 3 * c4), F32),
            dma((6,)),
            pltpu.SemaphoreType.REGULAR((max(1, groups - 2),)),
            dma((8,)), dma((8,)), dma((8,)),
            dma((1,)), dma((groups - 1,)), dma((1,)), dma((1,)), dma((groups - 1,)), dma((2, 1 + groups // 2)),
        ],
        compiler_params=pltpu.CompilerParams(
            collective_id=0, has_side_effects=True, vmem_limit_bytes=60 * 1024 * 1024
        ),
    )(vol, fine, down1, middle, shard, coarse_w)
    return result.reshape(c4, 1, cells)


def solution(mesh):
    placed = (
        P(None, "slab", "grp", None),
        P(),
        P(),
        P(),
        P(None, None, None, None, "grp"),
        P(None, None, None, None, "grp"),
    )
    body = functools.partial(per_device, mesh.shape["slab"], mesh.shape["grp"])
    return jax.shard_map(
        body, mesh=mesh, in_specs=placed, out_specs=P("grp", "slab", None), check_vma=False
    )
```
